32 devices in a mesh: row: 8 (over y, x, core), col: 4 (over z).
Axes of the slice: x: 2, y: 2, z: 4, core: 2. Of those that a mesh axis runs over, the one named last changes fastest.
Arguments:
- trailing: float32 [512, 512], P('row', 'col'), may hold values from -6 to 6
- panel_block: bfloat16 [512, 1024], P('row'), may hold values from -24 to 24
- diag_inverse: bfloat16 [1024, 1024], P('col'), as said below
- panel_points: float32 [20, 1024], replicated, may hold values from 0 to 1
- lengthscales: float32 [20], replicated, may hold values from 0.15 to 5
- targets: bfloat16 [1024], replicated, may hold values from -96 to 96
- base_a: float32 [20, 24576], P(None, 'row'), may hold values from 0 to 1
- base_b: float32 [20, 24576], P(None, 'row'), may hold values from 0 to 1
- pick_sets: int32 [96, 20], P('row'), may hold values 0 or 1
- cross_rhs: bfloat16 [512, 24576], P('col', 'row'), may hold values from -0.59765625 to 0.59765625
- mean_in: float32 [24576], P('row'), may hold values from -3 to 3
- var_in: float32 [24576], P('row'), may hold values from 1 to 2
Outputs:
- trailing_next: float32 [512, 512], P('row', 'col')
- cross_next: bfloat16 [512, 24576], P('col', 'row')
- post_mean: float32 [24576], P('row')
- post_variance: float32 [24576], P('row')
The draws below stay inside these ranges and needn't reach their ends.
Inputs may be any that keep to these rules, and one draw needn't show every extreme that they name: diag_inverse is lower triangular.
All inputs are finite; a program needn't handle non-finite values. No bound on the sum of `pick_sets` on one device may be relied on, other than what follows from the above.
Results may differ from the reference program's by a relative error of at most 0.0034.
Values may be sent and summed in bfloat16 or wider, within the bound.
No kernel may reach another device: no remote copies, remote signals or barrier semaphores. Data moves between devices by JAX's collectives and lax.ppermute only.
A program may use at most 64 MiB of HBM per device.

```python
import math
import jax
import jax.numpy as jnp
from jax import lax

PB = 1024
DIN = 20
BS = 16
QB = 256
M = 512
Q = 24576
NBLK = 96
N_ROW = 8
N_COL = 4


def draw_diag_inverse(key, part):
    first_key, second_key = jax.random.split(key)
    diagonal = jax.random.uniform(first_key, (PB,), jnp.float32, 1.0, 2.0) * PB ** (-0.5)
    below = jax.random.normal(second_key, (PB, PB), jnp.float32)
    below = below * (0.5 / PB)
    lower = jnp.tril(below, -1) + jnp.diag(diagonal)
    return lower.astype(jnp.bfloat16)


def draw_lengthscales(key, part):
    order_key, short_key, long_key = jax.random.split(key, 3)
    ranking = jax.random.permutation(order_key, DIN)
    relevant = ranking < 5
    short_scale = jnp.exp(jax.random.uniform(short_key, (DIN,), jnp.float32, math.log(0.2), math.log(0.45)))
    long_scale = jnp.exp(jax.random.uniform(long_key, (DIN,), jnp.float32, 0.0, math.log(5.0)))
    return jnp.where(relevant, short_scale, long_scale).astype(jnp.float32)


def touch_ends(drawn, rng, low, top_value):
    place = [jax.random.randint(jax.random.fold_in(rng, axis), (), 0, length) for axis, length in enumerate(drawn.shape)]
    widest = drawn.shape.index(max(drawn.shape))
    neighbour = place[:widest] + [(place[widest] + 1) % drawn.shape[widest]] + place[widest + 1:]
    return drawn.at[tuple(place)].set(low).at[tuple(neighbour)].set(top_value)


def block_scale(rng, shape, pieces, least, top_value):
    loudness, own = 1.0, jax.random.fold_in(rng, 6)
    for position, parts in pieces:
        draws = jnp.exp(jax.random.uniform(jax.random.fold_in(own, position), (parts,), jnp.float32, least / len(pieces), top_value / len(pieces)))
        loudness = loudness * jnp.repeat(draws, shape[position] // parts).reshape([-1 if axis == position else 1 for axis in range(len(shape))])
    return loudness


def scatter_about(stream_key, shape, scale, most, shards=(), dtype=jnp.bfloat16):
    array = jax.random.normal(stream_key, shape, jnp.float32) * scale
    if len(shards) > 0:
        array = block_scale(stream_key, shape, shards, -0.22, 0.18) * array
    return jnp.clip(array, min=-most, max=most).astype(dtype)


def setup_inputs(seed: int = 0) -> dict:
    streams_of = jax.random.split(jax.random.key(seed), 13)
    return {
        "trailing": scatter_about(streams_of[0], (M, M), 1.0, 6.0, ((0, 8), (1, 4)), jnp.float32),
        "panel_block": scatter_about(streams_of[1], (M, PB), 4.0, 24.0, ((0, 8),)),
        "diag_inverse": draw_diag_inverse(jax.random.fold_in(streams_of[12], 71), 0),
        "panel_points": jnp.clip(jax.random.uniform(streams_of[3], (DIN, PB), jnp.float32, 0.0, 1.0), 0.0, 1.0),
        "lengthscales": draw_lengthscales(jax.random.fold_in(streams_of[12], 71), 0),
        "targets": scatter_about(streams_of[5], (PB,), 16.0, 96.0),
        "base_a": jnp.clip(1.0 * jax.random.uniform(streams_of[6], (DIN, Q), jnp.float32) ** block_scale(streams_of[6], (DIN, Q), ((1, 8),), -0.2, 0.2), 0.0, 1.0),
        "base_b": jnp.clip(1.0 * jax.random.uniform(streams_of[7], (DIN, Q), jnp.float32) ** block_scale(streams_of[7], (DIN, Q), ((1, 8),), -0.2, 0.2), 0.0, 1.0),
        "pick_sets": touch_ends((jax.random.randint(streams_of[8], (NBLK, DIN), 0, 2) < 1).astype(jnp.int32), jax.random.fold_in(streams_of[8], 1), 0, 1),
        "cross_rhs": scatter_about(streams_of[9], (M, Q), 0.1, 0.59765625, ((0, 4), (1, 8))),
        "mean_in": scatter_about(streams_of[10], (Q,), 0.5, 3.0, ((0, 8),), jnp.float32),
        "var_in": jnp.clip(1.0 + 1.0 * jax.random.uniform(streams_of[11], (Q,), jnp.float32) ** block_scale(streams_of[11], (Q,), ((0, 8),), -0.2, 0.2), 1.0, 2.0),
    }


def cyclic_order(factor):
    shaped = factor.reshape(N_ROW, N_COL, BS, PB)
    return jnp.transpose(shaped, (1, 0, 2, 3)).reshape(M, PB)


def reference(trailing, panel_block, diag_inverse, panel_points, lengthscales, targets, base_a, base_b, pick_sets, cross_rhs, mean_in, var_in):
    factor = lax.dot_general(panel_block, diag_inverse, (((1,), (1,)), ((), ())), preferred_element_type=jnp.float32).astype(jnp.bfloat16)
    cyclic = cyclic_order(factor)
    trailing_next = trailing - lax.dot_general(factor, cyclic, (((1,), (1,)), ((), ())), preferred_element_type=jnp.float32)
    chosen = jnp.repeat(pick_sets, QB, axis=0).T
    scaled_points = panel_points / lengthscales[:, None]
    candidates = jnp.where(chosen == 1, base_b, base_a) / lengthscales[:, None]
    inner = lax.dot_general(scaled_points, candidates, (((0,), (0,)), ((), ())), precision=lax.Precision.HIGHEST, preferred_element_type=jnp.float32)
    distance = jnp.sum(scaled_points * scaled_points, axis=0)[:, None] + jnp.sum(candidates * candidates, axis=0)[None, :] - 2.0 * inner
    kernel_cols = jnp.exp(-0.5 * distance).astype(jnp.bfloat16)
    solves = jnp.dot(diag_inverse, kernel_cols, preferred_element_type=jnp.float32).astype(jnp.bfloat16)
    weights = jnp.dot(diag_inverse, targets, preferred_element_type=jnp.float32).astype(jnp.bfloat16)
    cross_next = (cross_rhs.astype(jnp.float32) - jnp.dot(cyclic, solves, preferred_element_type=jnp.float32)).astype(jnp.bfloat16)
    post_mean = mean_in + jnp.dot(weights, solves, preferred_element_type=jnp.float32)
    solved = solves.astype(jnp.float32)
    post_variance = var_in - jnp.sum(solved * solved, axis=0)
    return (trailing_next, cross_next, post_mean, post_variance)
```

```python
import functools
import math

import jax
import jax.numpy as jnp
from jax import lax
from jax.experimental import pallas as pl
from jax.experimental.pallas import tpu as pltpu
from jax.sharding import PartitionSpec as P

LOG2E = math.log2(math.e)
GROUP = 32
DEPTH = 8 * GROUP
LINK = jnp.float32
VMEM = pl.BlockSpec(memory_space=pltpu.VMEM)


def tile_of(n, most):
    while n % most:
        most //= 2
    return most


def column(row):
    n = row.shape[1]
    eye = lax.broadcasted_iota(jnp.int32, (n, n), 0) == lax.broadcasted_iota(jnp.int32, (n, n), 1)
    return jnp.sum(jnp.where(eye, row, jnp.zeros_like(row)), axis=1, keepdims=True)


def split3(x):
    first = x.astype(jnp.bfloat16).astype(jnp.float32)
    rest = x - first
    second = rest.astype(jnp.bfloat16).astype(jnp.float32)
    third = (rest - second).astype(jnp.bfloat16).astype(jnp.float32)
    return first, second, third


def pick_row(shape, rows):
    index = lax.broadcasted_iota(jnp.int32, shape, 0)
    out = jnp.zeros(shape, jnp.float32)
    for i, row in enumerate(rows):
        out = jnp.where(index == i, row, out)
    return out


def partial_kernel(n_col, swapped, panel_ref, inv_ref, *out_refs):
    rows = panel_ref.shape[0] // n_col
    me = lax.axis_index("col")
    inv = inv_ref[...]
    for d in range(n_col):
        block = me ^ d if swapped else d
        mine = panel_ref[pl.ds(block * rows, rows), :]
        slab = lax.dot_general(
            mine, inv, (((1,), (1,)), ((), ())), preferred_element_type=jnp.float32
        ).astype(jnp.bfloat16)
        part = jnp.dot(slab, inv, preferred_element_type=jnp.float32)
        if swapped:
            out_refs[d][...] = part.astype(out_refs[d].dtype)
        else:
            out_refs[0][d] = part.astype(out_refs[0].dtype)


def partial(panel, inv, n_col, swapped):
    rows, width = panel.shape[0] // n_col, panel.shape[1]
    if swapped:
        shapes = [jax.ShapeDtypeStruct((rows, width), jnp.float32 if d == 0 else LINK) for d in range(n_col)]
    else:
        shapes = [jax.ShapeDtypeStruct((n_col, rows, width), LINK)]
    return pl.pallas_call(
        functools.partial(partial_kernel, n_col, swapped),
        out_shape=shapes,
        in_specs=[VMEM] * 2,
        out_specs=[VMEM] * len(shapes),
        name="partial",
    )(panel, inv)


def columns_kernel(
    per_tile, points_ref, scale_ref, target_ref, pick_ref, a_ref, b_ref, inv_ref,
    k_ref, sums_ref, p32, pwide, pt, s32, st, inverse_scale, weight,
):
    din = points_ref.shape[0]
    depth = points_ref.shape[1]
    step = pl.program_id(0)

    @pl.when(step == 0)
    def _():
        inverse = 1.0 / column(scale_ref[...])
        inverse_scale[...] = inverse
        p32[...] = jnp.zeros_like(p32)
        s32[...] = jnp.zeros_like(s32)
        st[...] = jnp.zeros_like(st)
        p32[:din, :] = (points_ref[...] - 0.5) * inverse * LOG2E
        p = p32[...]
        first, second, third = split3(p)
        for g, part in enumerate((first, first, second, second, first, third)):
            pwide[g * GROUP : (g + 1) * GROUP, :] = part
        norm = (-0.5 / LOG2E) * jnp.sum(p * p, axis=0, keepdims=True)
        minus = jnp.full_like(norm, -1.0)
        pwide[6 * GROUP : 7 * GROUP, :] = pick_row((GROUP, depth), (minus, minus, minus) + split3(norm))
        pwide[7 * GROUP :, :] = jnp.zeros((GROUP, depth), jnp.float32)
        pt[...] = jnp.transpose(pwide[...]).astype(jnp.bfloat16)
        weight[...] = (
            jnp.sum(inv_ref[...].astype(jnp.float32) * target_ref[...].astype(jnp.float32), axis=1, keepdims=True)
            .astype(jnp.bfloat16)
            .astype(jnp.float32)
        )

    tile = a_ref.shape[1]
    wide = tile // per_tile
    for i in range(per_tile):
        chosen = column(pick_ref[pl.ds(step * per_tile + i, 1), :])
        here = pl.ds(i * wide, wide)
        s32[:din, here] = (jnp.where(chosen == 1, b_ref[:, here], a_ref[:, here]) - 0.5) * inverse_scale[...]
    s = s32[...]
    first, second, third = split3(s)
    for g, part in enumerate((first, second, first, second, third, first)):
        st[g * GROUP : (g + 1) * GROUP, :] = part.astype(jnp.bfloat16)
    norm = (0.5 * LOG2E) * jnp.sum(s * s, axis=0, keepdims=True)
    one = jnp.ones_like(norm)
    st[6 * GROUP : 7 * GROUP, :] = pick_row((GROUP, tile), split3(norm) + (one, one, one)).astype(jnp.bfloat16)

    chunk = min(256, depth)
    solve = None
    for m in range(depth // chunk):
        here = slice(m * chunk, (m + 1) * chunk)
        power = jnp.dot(pt[here, :], st[...], preferred_element_type=jnp.float32)
        k = jnp.exp2(power).astype(jnp.bfloat16)
        k_ref[here, :] = k
        term = jnp.dot(inv_ref[:, here], k, preferred_element_type=jnp.float32)
        solve = term if solve is None else solve + term
    solve = solve.astype(jnp.bfloat16).astype(jnp.float32)
    sums_ref[0:1, :] = jnp.sum(solve * weight[...], axis=0, keepdims=True)
    sums_ref[1:2, :] = jnp.sum(solve * solve, axis=0, keepdims=True)


def columns(points, scales, targets, base_a, base_b, picks, inv):
    din, depth = points.shape
    wide = base_a.shape[1]
    blocks = picks.shape[0]
    per_tile = 2 if blocks % 2 == 0 else 1
    tile = wide // blocks * per_tile
    slab = inv.shape[0]
    whole = lambda shape: pl.BlockSpec(shape, lambda i: (0, 0), pipeline_mode=pl.Buffered(1))
    moving = lambda rows: pl.BlockSpec((rows, tile), lambda i: (0, i))
    return pl.pallas_call(
        functools.partial(columns_kernel, per_tile),
        grid=(wide // tile,),
        out_shape=[
            jax.ShapeDtypeStruct((depth, wide), jnp.bfloat16),
            jax.ShapeDtypeStruct((2, wide), jnp.float32),
        ],
        in_specs=[
            whole((din, depth)), whole((1, din)), whole((1, depth)), whole((blocks, din)),
            moving(din), moving(din), whole((slab, depth)),
        ],
        out_specs=[moving(depth), moving(2)],
        scratch_shapes=[
            pltpu.VMEM((GROUP, depth), jnp.float32),
            pltpu.VMEM((DEPTH, depth), jnp.float32),
            pltpu.VMEM((depth, DEPTH), jnp.bfloat16),
            pltpu.VMEM((GROUP, tile), jnp.float32),
            pltpu.VMEM((DEPTH, tile), jnp.bfloat16),
            pltpu.VMEM((din, 1), jnp.float32),
            pltpu.VMEM((slab, 1), jnp.float32),
        ],
        compiler_params=pltpu.CompilerParams(vmem_limit_bytes=32 * 2**20),
        cost_estimate=pl.CostEstimate(
            flops=2 * depth * wide * (DEPTH + slab), bytes_accessed=2 * depth * wide, transcendentals=depth * wide
        ),
        name="columns",
    )(points, scales.reshape(1, din), targets.reshape(1, depth), picks, base_a, base_b, inv)


def update_kernel(places, n_in, *refs):
    blocks, (k_ref, rhs_ref, panel_ref, trailing_ref) = refs[:n_in], refs[n_in : n_in + 4]
    cross_ref, next_ref, left = refs[n_in + 4 :]
    rows = cross_ref.shape[0]

    @pl.when(pl.program_id(0) == 0)
    def _():
        me = lax.axis_index("row")
        for ref, place in zip(blocks, places):
            height = ref.shape[0]
            start = 0 if place is None else (me ^ place) * height
            full = ref[...].astype(jnp.float32)
            high = full.astype(jnp.bfloat16)
            left[0, pl.ds(start, height), :] = high
            left[1, pl.ds(start, height), :] = (full - high.astype(jnp.float32)).astype(jnp.bfloat16)
        panel = panel_ref[...]
        product = sum(
            lax.dot_general(panel, left[i], (((1,), (1,)), ((), ())), preferred_element_type=jnp.float32)
            for i in range(2)
        )
        next_ref[...] = trailing_ref[...] - product

    k = k_ref[...]
    product = jnp.dot(left[...].reshape(2 * rows, left.shape[2]), k, preferred_element_type=jnp.float32)
    cross_ref[...] = (
        rhs_ref[...].astype(jnp.float32) - (product[:rows] + product[rows:])
    ).astype(cross_ref.dtype)


def update(blocks, places, k, rhs, panel, trailing):
    depth, wide = k.shape
    rows = rhs.shape[0]
    tile = tile_of(wide, 512)
    whole = lambda x: pl.BlockSpec(x.shape, lambda i: (0, 0), pipeline_mode=pl.Buffered(1))
    moving = lambda rows: pl.BlockSpec((rows, tile), lambda i: (0, i))
    return pl.pallas_call(
        functools.partial(update_kernel, places, len(blocks)),
        grid=(wide // tile,),
        out_shape=[
            jax.ShapeDtypeStruct(rhs.shape, rhs.dtype),
            jax.ShapeDtypeStruct(trailing.shape, trailing.dtype),
        ],
        in_specs=[whole(b) for b in blocks] + [moving(depth), moving(rows), whole(panel), whole(trailing)],
        out_specs=[moving(rows), pl.BlockSpec(trailing.shape, lambda i: (0, 0))],
        scratch_shapes=[pltpu.VMEM((2, rows, depth), jnp.bfloat16)],
        compiler_params=pltpu.CompilerParams(vmem_limit_bytes=32 * 2**20),
        cost_estimate=pl.CostEstimate(
            flops=4 * rows * depth * wide, bytes_accessed=2 * depth * wide, transcendentals=0
        ),
        name="update",
    )(*blocks, k, rhs, panel, trailing)


def swap(x, axis, d):
    return lax.ppermute(x, axis, [(i, i ^ d) for i in range(lax.axis_size(axis))])


def local(
    trailing,
    panel_block,
    diag_inverse,
    panel_points,
    lengthscales,
    targets,
    base_a,
    base_b,
    pick_sets,
    cross_rhs,
    mean_in,
    var_in,
):
    n_row, n_col = lax.axis_size("row"), lax.axis_size("col")
    near = n_col in (2, 4)
    parts = partial(panel_block, diag_inverse, n_col, near)
    if near:
        got = [swap(parts[d], "col", d) for d in range(1, n_col)]
    k, sums = columns(panel_points, lengthscales, targets, base_a, base_b, pick_sets, diag_inverse)
    if near:
        reduced = parts[0]
        for x in got:
            reduced = reduced + x.astype(jnp.float32)
        totals = [sums] + [swap(sums, "col", d) for d in range(1, n_col)]
        total = sum(totals[1:], totals[0])
    else:
        reduced = lax.all_to_all(parts[0], "col", 0, 0).astype(jnp.float32).sum(0)
        total = lax.psum(sums, "col")
    reduced = reduced.astype(LINK)
    if n_row == 8:
        even = {0: reduced, **{d: swap(reduced, "row", d) for d in (2, 4, 6)}}
        odd = {d + 1: swap(x, "row", 1) for d, x in even.items()}
        both = {**even, **odd}
        places, blocks = tuple(both), list(both.values())
    else:
        places, blocks = (None,), [lax.all_gather(reduced, "row", axis=0, tiled=True)]
    cross_next, trailing_next = update(blocks, places, k, cross_rhs, panel_block, trailing)
    return trailing_next, cross_next, mean_in + total[0], var_in - total[1]


def solution(mesh):
    placed = (
        P("row", "col"),
        P("row", None),
        P("col", None),
        P(),
        P(),
        P(),
        P(None, "row"),
        P(None, "row"),
        P("row", None),
        P("col", "row"),
        P("row"),
        P("row"),
    )
    return jax.shard_map(
        local,
        mesh=mesh,
        in_specs=placed,
        out_specs=(P("row", "col"), P("col", "row"), P("row"), P("row")),
        check_vma=False,
    )
```

```python
import functools

import jax
import jax.numpy as jnp
from jax import lax
from jax.experimental import pallas as pl
from jax.experimental.pallas import tpu as pltpu
from jax.sharding import PartitionSpec as P

GROUP = 32
DEPTH = 8 * GROUP
LINK = jnp.float32
VMEM = pl.BlockSpec(memory_space=pltpu.VMEM)
HBM = pl.BlockSpec(memory_space=pltpu.HBM)


def in_hbm(*arrays):
    return [pltpu.with_memory_space_constraint(x, pltpu.HBM) for x in arrays]


def fetch(sources, targets, sems):
    copies = [pltpu.make_async_copy(s, t, sems.at[i]) for i, (s, t) in enumerate(zip(sources, targets))]
    for c in copies:
        c.start()
    return copies


def tile_of(n, most):
    while n % most:
        most //= 2
    return most


def column(row):
    n = row.shape[1]
    eye = lax.broadcasted_iota(jnp.int32, (n, n), 0) == lax.broadcasted_iota(jnp.int32, (n, n), 1)
    return jnp.sum(jnp.where(eye, row, jnp.zeros_like(row)), axis=1, keepdims=True)


def split3(x):
    first = x.astype(jnp.bfloat16).astype(jnp.float32)
    rest = x - first
    second = rest.astype(jnp.bfloat16).astype(jnp.float32)
    third = (rest - second).astype(jnp.bfloat16).astype(jnp.float32)
    return first, second, third


def pick_row(shape, rows):
    index = lax.broadcasted_iota(jnp.int32, shape, 0)
    out = jnp.zeros(shape, jnp.float32)
    for i, row in enumerate(rows):
        out = jnp.where(index == i, row, out)
    return out


def partial_kernel(n_col, swapped, panel_hbm, inv_hbm, *refs):
    out_refs, (panel_ref, inv_ref, sems) = refs[:-3], refs[-3:]
    copies = fetch((panel_hbm, inv_hbm), (panel_ref, inv_ref), sems)
    rows = panel_ref.shape[0] // n_col
    me = lax.axis_index("col")
    for c in copies:
        c.wait()
    inv = inv_ref[...]
    panel = panel_ref[...]
    if swapped:
        panel = jnp.concatenate([panel_ref[pl.ds((me ^ d) * rows, rows), :] for d in range(n_col)], axis=0)
    slab = lax.dot_general(
        panel, inv, (((1,), (1,)), ((), ())), preferred_element_type=jnp.float32
    ).astype(jnp.bfloat16)
    part = jnp.dot(slab, inv, preferred_element_type=jnp.float32)
    if swapped:
        for d in range(n_col):
            out_refs[d][...] = part[d * rows : (d + 1) * rows].astype(out_refs[d].dtype)
    else:
        out_refs[0][...] = part.reshape(out_refs[0].shape).astype(out_refs[0].dtype)


def partial(panel, inv, n_col, swapped):
    rows, width = panel.shape[0] // n_col, panel.shape[1]
    if swapped:
        shapes = [jax.ShapeDtypeStruct((rows, width), jnp.float32 if d == 0 else LINK) for d in range(n_col)]
    else:
        shapes = [jax.ShapeDtypeStruct((n_col, rows, width), LINK)]
    return pl.pallas_call(
        functools.partial(partial_kernel, n_col, swapped),
        out_shape=shapes,
        in_specs=[HBM] * 2,
        out_specs=[VMEM] * len(shapes),
        scratch_shapes=[pltpu.VMEM(x.shape, x.dtype) for x in (panel, inv)] + [pltpu.SemaphoreType.DMA((2,))],
        compiler_params=pltpu.CompilerParams(vmem_limit_bytes=16 * 2**20),
        name="partial",
    )(*in_hbm(panel, inv))


def columns_kernel(
    tile, points_hbm, scale_hbm, target_hbm, pick_hbm, a_hbm, b_hbm, inv_hbm,
    k_ref, sums_ref,
    points_ref, scale_ref, target_ref, pick_ref, a_ref, b_ref, inv_ref,
    p32, pwide, pt, s32, st, sems,
):
    copies = fetch(
        (points_hbm, scale_hbm, pick_hbm, a_hbm, b_hbm, inv_hbm, target_hbm),
        (points_ref, scale_ref, pick_ref, a_ref, b_ref, inv_ref, target_ref),
        sems,
    )
    din, depth = points_ref.shape
    wide = a_ref.shape[1]
    block = wide // pick_ref.shape[0]
    p32[...] = jnp.zeros_like(p32)
    s32[...] = jnp.zeros_like(s32)
    st[...] = jnp.zeros_like(st)
    for c in copies[:2]:
        c.wait()
    inverse = 1.0 / column(scale_ref[...])
    p32[:din, :] = (points_ref[...] - 0.5) * inverse
    p = p32[...]
    first, second, third = split3(p)
    for g, part in enumerate((first, first, second, second, first, third)):
        pwide[g * GROUP : (g + 1) * GROUP, :] = part
    norm = -0.5 * jnp.sum(p * p, axis=0, keepdims=True)
    minus = jnp.full_like(norm, -1.0)
    pwide[6 * GROUP : 7 * GROUP, :] = pick_row((GROUP, depth), (minus, minus, minus) + split3(norm))
    pwide[7 * GROUP :, :] = jnp.zeros((GROUP, depth), jnp.float32)
    pt[...] = jnp.transpose(pwide[...]).astype(jnp.bfloat16)
    for c in copies[2:]:
        c.wait()
    weight = (
        jnp.sum(inv_ref[...].astype(jnp.float32) * target_ref[...].astype(jnp.float32).reshape(1, depth), axis=1, keepdims=True)
        .astype(jnp.bfloat16)
        .astype(jnp.float32)
    )

    def step(t, carry):
        cols = pl.ds(t * tile, tile)
        for i in range(tile // block):
            chosen = column(pick_ref[pl.ds(t * (tile // block) + i, 1), :])
            here = pl.ds(t * tile + i * block, block)
            s32[:din, i * block : (i + 1) * block] = (
                jnp.where(chosen == 1, b_ref[:, here], a_ref[:, here]) - 0.5
            ) * inverse
        s = s32[...]
        first, second, third = split3(s)
        for g, part in enumerate((first, second, first, second, third, first)):
            st[g * GROUP : (g + 1) * GROUP, :] = part.astype(jnp.bfloat16)
        norm = 0.5 * jnp.sum(s * s, axis=0, keepdims=True)
        one = jnp.ones_like(norm)
        st[6 * GROUP : 7 * GROUP, :] = pick_row((GROUP, tile), split3(norm) + (one, one, one)).astype(jnp.bfloat16)
        power = jnp.dot(pt[...], st[...], preferred_element_type=jnp.float32)
        k = jnp.exp(power).astype(jnp.bfloat16)
        k_ref[:, cols] = k
        solve = jnp.dot(inv_ref[...], k, preferred_element_type=jnp.float32)
        solve = solve.astype(jnp.bfloat16).astype(jnp.float32)
        sums_ref[0:1, cols] = jnp.sum(solve * weight, axis=0, keepdims=True)
        sums_ref[1:2, cols] = jnp.sum(solve * solve, axis=0, keepdims=True)
        return carry

    lax.fori_loop(0, wide // tile, step, 0, unroll=True)


def columns(points, scales, targets, base_a, base_b, picks, inv):
    din, depth = points.shape
    wide = base_a.shape[1]
    blocks = picks.shape[0]
    tile = wide // blocks * (2 if blocks % 2 == 0 else 1)
    ins = (points, scales.reshape(1, din), targets, picks, base_a, base_b, inv)
    return pl.pallas_call(
        functools.partial(columns_kernel, tile),
        out_shape=[
            jax.ShapeDtypeStruct((depth, wide), jnp.bfloat16),
            jax.ShapeDtypeStruct((2, wide), jnp.float32),
        ],
        in_specs=[HBM] * len(ins),
        out_specs=[VMEM] * 2,
        scratch_shapes=[pltpu.VMEM(x.shape, x.dtype) for x in ins]
        + [
            pltpu.VMEM((GROUP, depth), jnp.float32),
            pltpu.VMEM((DEPTH, depth), jnp.float32),
            pltpu.VMEM((depth, DEPTH), jnp.bfloat16),
            pltpu.VMEM((GROUP, tile), jnp.float32),
            pltpu.VMEM((DEPTH, tile), jnp.bfloat16),
            pltpu.SemaphoreType.DMA((len(ins),)),
        ],
        compiler_params=pltpu.CompilerParams(vmem_limit_bytes=32 * 2**20),
        cost_estimate=pl.CostEstimate(
            flops=2 * depth * wide * (DEPTH + inv.shape[0]), bytes_accessed=2 * depth * wide, transcendentals=depth * wide
        ),
        name="columns",
    )(*in_hbm(*ins))


def update_kernel(places, tile, n_in, *refs):
    blocks, (k_ref, rhs_ref, panel_ref, trailing_ref) = refs[:n_in], refs[n_in : n_in + 4]
    cross_hbm, next_ref, left, cross, sems = refs[n_in + 4 :]
    rows, wide = rhs_ref.shape
    me = lax.axis_index("row")
    for ref, place in zip(blocks, places):
        height = ref.shape[0]
        start = 0 if place is None else (me ^ place) * height
        full = ref[...].astype(jnp.float32)
        high = full.astype(jnp.bfloat16)
        left[pl.ds(start, height), :] = high
        left[pl.ds(start + rows, height), :] = (full - high.astype(jnp.float32)).astype(jnp.bfloat16)
    copies = []
    for t in range(wide // tile):
        here = slice(t * tile, (t + 1) * tile)
        product = jnp.dot(left[...], k_ref[:, here], preferred_element_type=jnp.float32)
        cross[:, here] = (
            rhs_ref[:, here].astype(jnp.float32) - (product[:rows] + product[rows:])
        ).astype(cross.dtype)
        copies.append(pltpu.make_async_copy(cross.at[:, here], cross_hbm.at[:, here], sems.at[t]))
        copies[-1].start()
    product = lax.dot_general(
        panel_ref[...], left[...], (((1,), (1,)), ((), ())), preferred_element_type=jnp.float32
    )
    next_ref[...] = trailing_ref[...] - (product[:, :rows] + product[:, rows:])
    for c in copies:
        c.wait()


def update(blocks, places, k, rhs, panel, trailing):
    depth, wide = k.shape
    rows = rhs.shape[0]
    tile = tile_of(wide, 512)
    return pl.pallas_call(
        functools.partial(update_kernel, places, tile, len(blocks)),
        out_shape=[
            jax.ShapeDtypeStruct(rhs.shape, rhs.dtype),
            jax.ShapeDtypeStruct(trailing.shape, trailing.dtype),
        ],
        in_specs=[VMEM] * (len(blocks) + 4),
        out_specs=[HBM, VMEM],
        scratch_shapes=[
            pltpu.VMEM((2 * rows, depth), jnp.bfloat16),
            pltpu.VMEM(rhs.shape, rhs.dtype),
            pltpu.SemaphoreType.DMA((wide // tile,)),
        ],
        compiler_params=pltpu.CompilerParams(vmem_limit_bytes=32 * 2**20),
        cost_estimate=pl.CostEstimate(
            flops=4 * rows * depth * wide, bytes_accessed=2 * depth * wide, transcendentals=0
        ),
        name="update",
    )(*blocks, k, rhs, panel, trailing)


def finish_kernel(*refs):
    parts, (mean_ref, var_ref, out_mean, out_var) = refs[:-4], refs[-4:]
    total = parts[0][...]
    for x in parts[1:]:
        total = total + x[...]
    out_mean[...] = mean_ref[...] + total[0:1]
    out_var[...] = var_ref[...] - total[1:2]


def finish(parts, mean, var):
    wide = mean.shape[0]
    flat = jax.ShapeDtypeStruct((1, wide), jnp.float32)
    out_mean, out_var = pl.pallas_call(
        finish_kernel,
        out_shape=[flat, flat],
        in_specs=[VMEM] * (len(parts) + 2),
        out_specs=[VMEM] * 2,
        compiler_params=pltpu.CompilerParams(vmem_limit_bytes=8 * 2**20),
        name="finish",
    )(*parts, mean.reshape(1, wide), var.reshape(1, wide))
    return out_mean.reshape(wide), out_var.reshape(wide)


def swap(x, axis, d):
    return lax.ppermute(x, axis, [(i, i ^ d) for i in range(lax.axis_size(axis))])


def local(
    trailing,
    panel_block,
    diag_inverse,
    panel_points,
    lengthscales,
    targets,
    base_a,
    base_b,
    pick_sets,
    cross_rhs,
    mean_in,
    var_in,
):
    n_row, n_col = lax.axis_size("row"), lax.axis_size("col")
    near = n_col in (2, 4)
    parts = partial(panel_block, diag_inverse, n_col, near)
    if near:
        got = [swap(parts[d], "col", d) for d in range(1, n_col)]
    k, sums = columns(panel_points, lengthscales, targets, base_a, base_b, pick_sets, diag_inverse)
    if near:
        got, k, sums = lax.optimization_barrier((got, k, sums))
        reduced = parts[0]
        for x in got:
            reduced = reduced + x.astype(jnp.float32)
        totals = [sums] + [swap(sums, "col", d) for d in range(1, n_col)]
    else:
        reduced = lax.all_to_all(parts[0], "col", 0, 0).astype(jnp.float32).sum(0)
        totals = [lax.psum(sums, "col")]
    reduced = reduced.astype(LINK)
    if n_row == 8:
        even = {0: reduced, **{d: swap(reduced, "row", d) for d in (2, 4, 6)}}
        odd = {d + 1: swap(x, "row", 1) for d, x in even.items()}
        both = {**even, **odd}
        places, blocks = tuple(both), list(both.values())
    else:
        places, blocks = (None,), [lax.all_gather(reduced, "row", axis=0, tiled=True)]
    cross_next, trailing_next = update(blocks, places, k, cross_rhs, panel_block, trailing)
    cross_next, totals = lax.optimization_barrier((cross_next, totals))
    return trailing_next, cross_next, *finish(totals, mean_in, var_in)


def solution(mesh):
    placed = (
        P("row", "col"),
        P("row", None),
        P("col", None),
        P(),
        P(),
        P(),
        P(None, "row"),
        P(None, "row"),
        P("row", None),
        P("col", "row"),
        P("row"),
        P("row"),
    )
    return jax.shard_map(
        local,
        mesh=mesh,
        in_specs=placed,
        out_specs=(P("row", "col"), P("col", "row"), P("row"), P("row")),
        check_vma=False,
    )
```

```python
import functools

import jax
import jax.numpy as jnp
from jax import lax
from jax.experimental import pallas as pl
from jax.experimental.pallas import tpu as pltpu
from jax.sharding import PartitionSpec as P

GROUP = 32
DEPTH = 8 * GROUP
LINK = jnp.bfloat16
VMEM = pl.BlockSpec(memory_space=pltpu.VMEM)
HBM = pl.BlockSpec(memory_space=pltpu.HBM)


def in_hbm(*arrays):
    return [pltpu.with_memory_space_constraint(x, pltpu.HBM) for x in arrays]


def fetch(sources, targets, sems):
    copies = [pltpu.make_async_copy(s, t, sems.at[i]) for i, (s, t) in enumerate(zip(sources, targets))]
    for c in copies:
        c.start()
    return copies


def tile_of(n, most):
    while n % most:
        most //= 2
    return most


def column(row):
    n = row.shape[1]
    eye = lax.broadcasted_iota(jnp.int32, (n, n), 0) == lax.broadcasted_iota(jnp.int32, (n, n), 1)
    return jnp.sum(jnp.where(eye, row, jnp.zeros_like(row)), axis=1, keepdims=True)


def split3(x):
    first = x.astype(jnp.bfloat16).astype(jnp.float32)
    rest = x - first
    second = rest.astype(jnp.bfloat16).astype(jnp.float32)
    third = (rest - second).astype(jnp.bfloat16).astype(jnp.float32)
    return first, second, third


def pick_row(shape, rows):
    index = lax.broadcasted_iota(jnp.int32, shape, 0)
    out = jnp.zeros(shape, jnp.float32)
    for i, row in enumerate(rows):
        out = jnp.where(index == i, row, out)
    return out


def partial_kernel(n_col, swapped, n_more, *refs):
    sources, refs = refs[: 2 + n_more], refs[2 + n_more :]
    more, out_refs, (panel_ref, sems) = refs[: n_more + 1], refs[n_more + 1 : -2], refs[-2:]
    inv_ref = more[0]
    copies = fetch(sources, (panel_ref, *more), sems)
    rows = panel_ref.shape[0] // n_col
    me = lax.axis_index("col")
    for c in copies[:2]:
        c.wait()
    inv = inv_ref[...]
    panel = panel_ref[...]
    if swapped:
        panel = jnp.concatenate([panel_ref[pl.ds((me ^ d) * rows, rows), :] for d in range(n_col)], axis=0)
    slab = lax.dot_general(
        panel, inv, (((1,), (1,)), ((), ())), preferred_element_type=jnp.float32
    ).astype(jnp.bfloat16)
    part = jnp.dot(slab, inv, preferred_element_type=jnp.float32)
    if swapped:
        for d in range(n_col):
            out_refs[d][...] = part[d * rows : (d + 1) * rows].astype(out_refs[d].dtype)
    else:
        out_refs[0][...] = part.reshape(out_refs[0].shape).astype(out_refs[0].dtype)
    for c in copies[2:]:
        c.wait()


def partial(panel, inv, more, n_col, swapped):
    rows, width = panel.shape[0] // n_col, panel.shape[1]
    shapes = [jax.ShapeDtypeStruct(x.shape, x.dtype) for x in (inv, *more)]
    if swapped:
        shapes += [jax.ShapeDtypeStruct((rows, width), jnp.float32 if d == 0 else LINK) for d in range(n_col)]
    else:
        shapes += [jax.ShapeDtypeStruct((n_col, rows, width), LINK)]
    out = pl.pallas_call(
        functools.partial(partial_kernel, n_col, swapped, len(more)),
        out_shape=shapes,
        in_specs=[HBM] * (2 + len(more)),
        out_specs=[VMEM] * len(shapes),
        scratch_shapes=[pltpu.VMEM(panel.shape, panel.dtype), pltpu.SemaphoreType.DMA((2 + len(more),))],
        compiler_params=pltpu.CompilerParams(vmem_limit_bytes=16 * 2**20),
        name="partial",
    )(*in_hbm(panel, inv, *more))
    return out[: 1 + len(more)], out[1 + len(more) :]


def columns_kernel(
    tile, inv_ref, points_ref, scale_ref, target_ref, pick_ref, a_ref, b_ref,
    k_ref, sums_ref, p32, pwide, pt, s32, st,
):
    din, depth = points_ref.shape
    wide = a_ref.shape[1]
    block = wide // pick_ref.shape[0]
    p32[...] = jnp.zeros_like(p32)
    s32[...] = jnp.zeros_like(s32)
    st[...] = jnp.zeros_like(st)
    inverse = 1.0 / column(scale_ref[...])
    p32[:din, :] = (points_ref[...] - 0.5) * inverse
    p = p32[...]
    first, second, third = split3(p)
    for g, part in enumerate((first, first, second, second, first, third)):
        pwide[g * GROUP : (g + 1) * GROUP, :] = part
    norm = -0.5 * jnp.sum(p * p, axis=0, keepdims=True)
    minus = jnp.full_like(norm, -1.0)
    pwide[6 * GROUP : 7 * GROUP, :] = pick_row((GROUP, depth), (minus, minus, minus) + split3(norm))
    pwide[7 * GROUP :, :] = jnp.zeros((GROUP, depth), jnp.float32)
    pt[...] = jnp.transpose(pwide[...]).astype(jnp.bfloat16)
    weight = (
        jnp.sum(inv_ref[...].astype(jnp.float32) * target_ref[...].astype(jnp.float32).reshape(1, depth), axis=1, keepdims=True)
        .astype(jnp.bfloat16)
        .astype(jnp.float32)
    )

    def step(t, carry):
        cols = pl.ds(t * tile, tile)
        for i in range(tile // block):
            chosen = column(pick_ref[pl.ds(t * (tile // block) + i, 1), :])
            here = pl.ds(t * tile + i * block, block)
            s32[:din, i * block : (i + 1) * block] = (
                jnp.where(chosen == 1, b_ref[:, here], a_ref[:, here]) - 0.5
            ) * inverse
        s = s32[...]
        first, second, third = split3(s)
        for g, part in enumerate((first, second, first, second, third, first)):
            st[g * GROUP : (g + 1) * GROUP, :] = part.astype(jnp.bfloat16)
        norm = 0.5 * jnp.sum(s * s, axis=0, keepdims=True)
        one = jnp.ones_like(norm)
        st[6 * GROUP : 7 * GROUP, :] = pick_row((GROUP, tile), split3(norm) + (one, one, one)).astype(jnp.bfloat16)
        power = jnp.dot(pt[...], st[...], preferred_element_type=jnp.float32)
        k = jnp.exp(power).astype(jnp.bfloat16)
        k_ref[:, cols] = k
        solve = jnp.dot(inv_ref[...], k, preferred_element_type=jnp.float32)
        solve = solve.astype(jnp.bfloat16).astype(jnp.float32)
        sums_ref[0:1, cols] = jnp.sum(solve * weight, axis=0, keepdims=True)
        sums_ref[1:2, cols] = jnp.sum(solve * solve, axis=0, keepdims=True)
        return carry

    lax.fori_loop(0, wide // tile, step, 0, unroll=True)


def columns(ins):
    inv, points, _, _, picks, base, _ = ins
    depth, wide, blocks = points.shape[1], base.shape[1], picks.shape[0]
    tile = wide // blocks * (2 if blocks % 2 == 0 else 1)
    return pl.pallas_call(
        functools.partial(columns_kernel, tile),
        out_shape=[
            jax.ShapeDtypeStruct((depth, wide), jnp.bfloat16),
            jax.ShapeDtypeStruct((2, wide), jnp.float32),
        ],
        in_specs=[VMEM] * len(ins),
        out_specs=[VMEM] * 2,
        scratch_shapes=[
            pltpu.VMEM((GROUP, depth), jnp.float32),
            pltpu.VMEM((DEPTH, depth), jnp.float32),
            pltpu.VMEM((depth, DEPTH), jnp.bfloat16),
            pltpu.VMEM((GROUP, tile), jnp.float32),
            pltpu.VMEM((DEPTH, tile), jnp.bfloat16),
        ],
        compiler_params=pltpu.CompilerParams(vmem_limit_bytes=32 * 2**20),
        cost_estimate=pl.CostEstimate(
            flops=2 * depth * wide * (DEPTH + inv.shape[0]), bytes_accessed=2 * depth * wide, transcendentals=depth * wide
        ),
        name="columns",
    )(*ins)


def update_kernel(places, tile, n_in, *refs):
    blocks, (k_ref, rhs_ref, panel_ref, trailing_ref) = refs[:n_in], refs[n_in : n_in + 4]
    cross_hbm, next_ref, left, cross, sems = refs[n_in + 4 :]
    rows, wide = rhs_ref.shape
    me = lax.axis_index("row")
    for ref, place in zip(blocks, places):
        height = ref.shape[0] // len(place)
        for i, xor in enumerate(place):
            start = 0 if xor is None else (me ^ xor) * height
            left[pl.ds(start, height), :] = ref[i * height : (i + 1) * height, :]
    copies = []
    for t in range(wide // tile):
        here = slice(t * tile, (t + 1) * tile)
        product = jnp.dot(left[...], k_ref[:, here], preferred_element_type=jnp.float32)
        cross[:, here] = (rhs_ref[:, here].astype(jnp.float32) - product).astype(cross.dtype)
        copies.append(pltpu.make_async_copy(cross.at[:, here], cross_hbm.at[:, here], sems.at[t]))
        copies[-1].start()
    product = lax.dot_general(
        panel_ref[...], left[...], (((1,), (1,)), ((), ())), preferred_element_type=jnp.float32
    )
    next_ref[...] = trailing_ref[...] - product
    for c in copies:
        c.wait()


def update(blocks, places, k, rhs, panel, trailing):
    depth, wide = k.shape
    rows = rhs.shape[0]
    tile = tile_of(wide, 512)
    return pl.pallas_call(
        functools.partial(update_kernel, places, tile, len(blocks)),
        out_shape=[
            jax.ShapeDtypeStruct(rhs.shape, rhs.dtype),
            jax.ShapeDtypeStruct(trailing.shape, trailing.dtype),
        ],
        in_specs=[VMEM] * (len(blocks) + 4),
        out_specs=[HBM, VMEM],
        scratch_shapes=[
            pltpu.VMEM((rows, depth), jnp.bfloat16),
            pltpu.VMEM(rhs.shape, rhs.dtype),
            pltpu.SemaphoreType.DMA((wide // tile,)),
        ],
        compiler_params=pltpu.CompilerParams(vmem_limit_bytes=32 * 2**20),
        cost_estimate=pl.CostEstimate(
            flops=2 * rows * depth * wide, bytes_accessed=2 * depth * wide, transcendentals=0
        ),
        name="update",
    )(*blocks, k, rhs, panel, trailing)


def finish_kernel(*refs):
    parts, (mean_ref, var_ref, out_mean, out_var) = refs[:-4], refs[-4:]
    total = parts[0][...]
    for x in parts[1:]:
        total = total + x[...]
    out_mean[...] = mean_ref[...] + total[0:1]
    out_var[...] = var_ref[...] - total[1:2]


def finish(parts, mean, var):
    wide = mean.shape[0]
    flat = jax.ShapeDtypeStruct((1, wide), jnp.float32)
    out_mean, out_var = pl.pallas_call(
        finish_kernel,
        out_shape=[flat, flat],
        in_specs=[VMEM] * (len(parts) + 2),
        out_specs=[VMEM] * 2,
        compiler_params=pltpu.CompilerParams(vmem_limit_bytes=8 * 2**20),
        name="finish",
    )(*parts, mean.reshape(1, wide), var.reshape(1, wide))
    return out_mean.reshape(wide), out_var.reshape(wide)


def swap(x, axis, d):
    return lax.ppermute(x, axis, [(i, i ^ d) for i in range(lax.axis_size(axis))])


def local(
    trailing,
    panel_block,
    diag_inverse,
    panel_points,
    lengthscales,
    targets,
    base_a,
    base_b,
    pick_sets,
    cross_rhs,
    mean_in,
    var_in,
):
    n_row, n_col = lax.axis_size("row"), lax.axis_size("col")
    near = n_col in (2, 4)
    more = (panel_points, lengthscales.reshape(1, -1), targets, pick_sets, base_a, base_b)
    ins, parts = partial(panel_block, diag_inverse, more, n_col, near)
    if near:
        got = [swap(parts[d], "col", d) for d in range(1, n_col)]
    k, sums = columns(ins)
    if near:
        got, k, sums = lax.optimization_barrier((got, k, sums))
        reduced = parts[0]
        for x in got:
            reduced = reduced + x.astype(jnp.float32)
        totals = [sums] + [swap(sums, "col", d) for d in range(1, n_col)]
    else:
        reduced = lax.all_to_all(parts[0], "col", 0, 0).astype(jnp.float32).sum(0)
        totals = [lax.psum(sums, "col")]
    reduced = reduced.astype(LINK)
    if n_row == 8:
        pair = jnp.concatenate([reduced, swap(reduced, "row", 1)], axis=0)
        blocks = [pair] + [swap(pair, "row", d) for d in (2, 4, 6)]
        places = [(d, d + 1) for d in (0, 2, 4, 6)]
    else:
        blocks, places = [lax.all_gather(reduced, "row", axis=0, tiled=True)], [(None,)]
    cross_next, trailing_next = update(blocks, places, k, cross_rhs, panel_block, trailing)
    cross_next, totals = lax.optimization_barrier((cross_next, totals))
    return trailing_next, cross_next, *finish(totals, mean_in, var_in)


def solution(mesh):
    placed = (
        P("row", "col"),
        P("row", None),
        P("col", None),
        P(),
        P(),
        P(),
        P(None, "row"),
        P(None, "row"),
        P("row", None),
        P("col", "row"),
        P("row"),
        P("row"),
    )
    return jax.shard_map(
        local,
        mesh=mesh,
        in_specs=placed,
        out_specs=(P("row", "col"), P("col", "row"), P("row"), P("row")),
        check_vma=False,
    )
```

```python
import functools

import jax
import jax.numpy as jnp
from jax import lax
from jax.experimental import pallas as pl
from jax.experimental.pallas import tpu as pltpu
from jax.sharding import PartitionSpec as P

GROUP = 32
DEPTH = 8 * GROUP
LINK = jnp.bfloat16
VMEM = pl.BlockSpec(memory_space=pltpu.VMEM)
HBM = pl.BlockSpec(memory_space=pltpu.HBM)


def in_hbm(*arrays):
    return [pltpu.with_memory_space_constraint(x, pltpu.HBM) for x in arrays]


def fetch(sources, targets, sems):
    copies = [pltpu.make_async_copy(s, t, sems.at[i]) for i, (s, t) in enumerate(zip(sources, targets))]
    for c in copies:
        c.start()
    return copies


def tile_of(n, most):
    while n % most:
        most //= 2
    return most


def column(row):
    n = row.shape[1]
    eye = lax.broadcasted_iota(jnp.int32, (n, n), 0) == lax.broadcasted_iota(jnp.int32, (n, n), 1)
    return jnp.sum(jnp.where(eye, row, jnp.zeros_like(row)), axis=1, keepdims=True)


def split3(x):
    first = x.astype(jnp.bfloat16).astype(jnp.float32)
    rest = x - first
    second = rest.astype(jnp.bfloat16).astype(jnp.float32)
    third = (rest - second).astype(jnp.bfloat16).astype(jnp.float32)
    return first, second, third


def pick_row(shape, rows):
    index = lax.broadcasted_iota(jnp.int32, shape, 0)
    out = jnp.zeros(shape, jnp.float32)
    for i, row in enumerate(rows):
        out = jnp.where(index == i, row, out)
    return out


def partial_kernel(n_col, swapped, n_more, *refs):
    sources, refs = refs[: 2 + n_more], refs[2 + n_more :]
    more, out_refs, (panel_ref, sems) = refs[: n_more + 1], refs[n_more + 1 : -2], refs[-2:]
    inv_ref = more[0]
    copies = fetch(sources, (panel_ref, *more), sems)
    rows = panel_ref.shape[0] // n_col
    me = lax.axis_index("col")
    for c in copies[:2]:
        c.wait()
    inv = inv_ref[...]
    panel = panel_ref[...]
    if swapped:
        panel = jnp.concatenate([panel_ref[pl.ds((me ^ d) * rows, rows), :] for d in range(n_col)], axis=0)
    slab = lax.dot_general(
        panel, inv, (((1,), (1,)), ((), ())), preferred_element_type=jnp.float32
    ).astype(jnp.bfloat16)
    part = jnp.dot(slab, inv, preferred_element_type=jnp.float32)
    if swapped:
        for d in range(n_col):
            out_refs[d][...] = part[d * rows : (d + 1) * rows].astype(out_refs[d].dtype)
    else:
        out_refs[0][...] = part.reshape(out_refs[0].shape).astype(out_refs[0].dtype)
    for c in copies[2:]:
        c.wait()


def partial(panel, inv, more, n_col, swapped):
    rows, width = panel.shape[0] // n_col, panel.shape[1]
    shapes = [jax.ShapeDtypeStruct(x.shape, x.dtype) for x in (inv, *more)]
    if swapped:
        shapes += [jax.ShapeDtypeStruct((rows, width), jnp.float32 if d == 0 else LINK) for d in range(n_col)]
    else:
        shapes += [jax.ShapeDtypeStruct((n_col, rows, width), LINK)]
    out = pl.pallas_call(
        functools.partial(partial_kernel, n_col, swapped, len(more)),
        out_shape=shapes,
        in_specs=[HBM] * (2 + len(more)),
        out_specs=[VMEM] * len(shapes),
        scratch_shapes=[pltpu.VMEM(panel.shape, panel.dtype), pltpu.SemaphoreType.DMA((2 + len(more),))],
        compiler_params=pltpu.CompilerParams(vmem_limit_bytes=16 * 2**20),
        name="partial",
    )(*in_hbm(panel, inv, *more))
    return out[: 1 + len(more)], out[1 + len(more) :]


def columns_kernel(
    tile, inv_ref, points_ref, scale_ref, target_ref, pick_ref, a_ref, b_ref,
    k_ref, sums_ref, p32, pwide, pt, s32, st,
):
    din, depth = points_ref.shape
    wide = a_ref.shape[1]
    block = wide // pick_ref.shape[0]
    p32[...] = jnp.zeros_like(p32)
    s32[...] = jnp.zeros_like(s32)
    st[...] = jnp.zeros_like(st)
    inverse = 1.0 / column(scale_ref[...])
    p32[:din, :] = (points_ref[...] - 0.5) * inverse
    p = p32[...]
    first, second, third = split3(p)
    for g, part in enumerate((first, first, second, second, first, third)):
        pwide[g * GROUP : (g + 1) * GROUP, :] = part
    norm = -0.5 * jnp.sum(p * p, axis=0, keepdims=True)
    minus = jnp.full_like(norm, -1.0)
    pwide[6 * GROUP : 7 * GROUP, :] = pick_row((GROUP, depth), (minus, minus, minus) + split3(norm))
    pwide[7 * GROUP :, :] = jnp.zeros((GROUP, depth), jnp.float32)
    pt[...] = jnp.transpose(pwide[...]).astype(jnp.bfloat16)
    weight = (
        jnp.sum(inv_ref[...].astype(jnp.float32) * target_ref[...].astype(jnp.float32).reshape(1, depth), axis=1, keepdims=True)
        .astype(jnp.bfloat16)
        .astype(jnp.float32)
    )

    def step(t, carry):
        cols = pl.ds(t * tile, tile)
        for i in range(tile // block):
            chosen = column(pick_ref[pl.ds(t * (tile // block) + i, 1), :])
            here = pl.ds(t * tile + i * block, block)
            s32[:din, i * block : (i + 1) * block] = (
                jnp.where(chosen == 1, b_ref[:, here], a_ref[:, here]) - 0.5
            ) * inverse
        s = s32[...]
        first, second, third = split3(s)
        for g, part in enumerate((first, second, first, second, third, first)):
            st[g * GROUP : (g + 1) * GROUP, :] = part.astype(jnp.bfloat16)
        norm = 0.5 * jnp.sum(s * s, axis=0, keepdims=True)
        one = jnp.ones_like(norm)
        st[6 * GROUP : 7 * GROUP, :] = pick_row((GROUP, tile), split3(norm) + (one, one, one)).astype(jnp.bfloat16)
        power = jnp.dot(pt[...], st[...], preferred_element_type=jnp.float32)
        k = jnp.exp(power).astype(jnp.bfloat16)
        k_ref[:, cols] = k
        solve = jnp.dot(inv_ref[...], k, preferred_element_type=jnp.float32)
        solve = solve.astype(jnp.bfloat16).astype(jnp.float32)
        sums_ref[0:1, cols] = jnp.sum(solve * weight, axis=0, keepdims=True)
        sums_ref[1:2, cols] = jnp.sum(solve * solve, axis=0, keepdims=True)
        return carry

    lax.fori_loop(0, wide // tile, step, 0, unroll=True)


def columns(ins):
    inv, points, _, _, picks, base, _ = ins
    depth, wide, blocks = points.shape[1], base.shape[1], picks.shape[0]
    tile = wide // blocks * (2 if blocks % 2 == 0 else 1)
    return pl.pallas_call(
        functools.partial(columns_kernel, tile),
        out_shape=[
            jax.ShapeDtypeStruct((depth, wide), jnp.bfloat16),
            jax.ShapeDtypeStruct((2, wide), jnp.float32),
        ],
        in_specs=[VMEM] * len(ins),
        out_specs=[VMEM] * 2,
        scratch_shapes=[
            pltpu.VMEM((GROUP, depth), jnp.float32),
            pltpu.VMEM((DEPTH, depth), jnp.float32),
            pltpu.VMEM((depth, DEPTH), jnp.bfloat16),
            pltpu.VMEM((GROUP, tile), jnp.float32),
            pltpu.VMEM((DEPTH, tile), jnp.bfloat16),
        ],
        compiler_params=pltpu.CompilerParams(vmem_limit_bytes=32 * 2**20),
        cost_estimate=pl.CostEstimate(
            flops=2 * depth * wide * (DEPTH + inv.shape[0]), bytes_accessed=2 * depth * wide, transcendentals=depth * wide
        ),
        name="columns",
    )(*ins)


def update_kernel(places, cuts, n_in, *refs):
    blocks, (k_ref, rhs_ref, panel_ref, trailing_ref) = refs[:n_in], refs[n_in : n_in + 4]
    cross_hbm, next_hbm, left, cross, following, sems = refs[n_in + 4 :]
    rows, wide = rhs_ref.shape
    me = lax.axis_index("row")
    for ref, place in zip(blocks, places):
        height = ref.shape[0] // len(place)
        for i, xor in enumerate(place):
            start = 0 if xor is None else (me ^ xor) * height
            left[pl.ds(start, height), :] = ref[i * height : (i + 1) * height, :]
    product = lax.dot_general(
        panel_ref[...], left[...], (((1,), (1,)), ((), ())), preferred_element_type=jnp.float32
    )
    following[...] = trailing_ref[...] - product
    copies = [pltpu.make_async_copy(following, next_hbm, sems.at[len(cuts)])]
    copies[0].start()
    for t, (start, stop) in enumerate(cuts):
        product = jnp.dot(left[...], k_ref[:, start:stop], preferred_element_type=jnp.float32)
        cross[:, start:stop] = (rhs_ref[:, start:stop].astype(jnp.float32) - product).astype(cross.dtype)
        copies.append(pltpu.make_async_copy(cross.at[:, start:stop], cross_hbm.at[:, start:stop], sems.at[t]))
        copies[-1].start()
    for c in copies:
        c.wait()


def update(blocks, places, k, rhs, panel, trailing):
    depth, wide = k.shape
    rows = rhs.shape[0]
    tile = tile_of(wide, 512)
    edges = list(range(0, wide, tile)) + [wide - tile // 2, wide]
    cuts = list(zip(edges, edges[1:]))
    return pl.pallas_call(
        functools.partial(update_kernel, places, cuts, len(blocks)),
        out_shape=[
            jax.ShapeDtypeStruct(rhs.shape, rhs.dtype),
            jax.ShapeDtypeStruct(trailing.shape, trailing.dtype),
        ],
        in_specs=[VMEM] * (len(blocks) + 4),
        out_specs=[HBM, HBM],
        scratch_shapes=[
            pltpu.VMEM((rows, depth), jnp.bfloat16),
            pltpu.VMEM(rhs.shape, rhs.dtype),
            pltpu.VMEM(trailing.shape, trailing.dtype),
            pltpu.SemaphoreType.DMA((len(cuts) + 1,)),
        ],
        compiler_params=pltpu.CompilerParams(vmem_limit_bytes=32 * 2**20),
        cost_estimate=pl.CostEstimate(
            flops=2 * rows * depth * wide, bytes_accessed=2 * depth * wide, transcendentals=0
        ),
        name="update",
    )(*blocks, k, rhs, panel, trailing)


def finish_kernel(*refs):
    parts, (mean_ref, var_ref, out_mean, out_var) = refs[:-4], refs[-4:]
    total = parts[0][...]
    for x in parts[1:]:
        total = total + x[...]
    out_mean[...] = mean_ref[...] + total[0:1]
    out_var[...] = var_ref[...] - total[1:2]


def finish(parts, mean, var):
    wide = mean.shape[0]
    flat = jax.ShapeDtypeStruct((1, wide), jnp.float32)
    out_mean, out_var = pl.pallas_call(
        finish_kernel,
        out_shape=[flat, flat],
        in_specs=[VMEM] * (len(parts) + 2),
        out_specs=[VMEM] * 2,
        compiler_params=pltpu.CompilerParams(vmem_limit_bytes=8 * 2**20),
        name="finish",
    )(*parts, mean.reshape(1, wide), var.reshape(1, wide))
    return out_mean.reshape(wide), out_var.reshape(wide)


def swap(x, axis, d):
    return lax.ppermute(x, axis, [(i, i ^ d) for i in range(lax.axis_size(axis))])


def local(
    trailing,
    panel_block,
    diag_inverse,
    panel_points,
    lengthscales,
    targets,
    base_a,
    base_b,
    pick_sets,
    cross_rhs,
    mean_in,
    var_in,
):
    n_row, n_col = lax.axis_size("row"), lax.axis_size("col")
    near = n_col in (2, 4)
    more = (panel_points, lengthscales.reshape(1, -1), targets, pick_sets, base_a, base_b)
    ins, parts = partial(panel_block, diag_inverse, more, n_col, near)
    if near:
        got = [swap(parts[d], "col", d) for d in range(n_col - 1, 0, -1)]
    k, sums = columns(ins)
    if near:
        got, k, sums = lax.optimization_barrier((got, k, sums))
        reduced = parts[0]
        for x in got:
            reduced = reduced + x.astype(jnp.float32)
        totals = [sums] + [swap(sums, "col", d) for d in range(1, n_col)]
    else:
        reduced = lax.all_to_all(parts[0], "col", 0, 0).astype(jnp.float32).sum(0)
        totals = [lax.psum(sums, "col")]
    reduced = reduced.astype(LINK)
    if n_row == 8:
        pair = jnp.concatenate([reduced, swap(reduced, "row", 1)], axis=0)
        blocks = [pair] + [swap(pair, "row", d) for d in (2, 4, 6)]
        places = [(d, d + 1) for d in (0, 2, 4, 6)]
    else:
        blocks, places = [lax.all_gather(reduced, "row", axis=0, tiled=True)], [(None,)]
    cross_next, trailing_next = update(blocks, places, k, cross_rhs, panel_block, trailing)
    cross_next, totals = lax.optimization_barrier((cross_next, totals))
    return trailing_next, cross_next, *finish(totals, mean_in, var_in)


def solution(mesh):
    placed = (
        P("row", "col"),
        P("row", None),
        P("col", None),
        P(),
        P(),
        P(),
        P(None, "row"),
        P(None, "row"),
        P("row", None),
        P("col", "row"),
        P("row"),
        P("row"),
    )
    return jax.shard_map(
        local,
        mesh=mesh,
        in_specs=placed,
        out_specs=(P("row", "col"), P("col", "row"), P("row"), P("row")),
        check_vma=False,
    )
```

```python
import functools

import jax
import jax.numpy as jnp
from jax import lax
from jax.experimental import pallas as pl
from jax.experimental.pallas import tpu as pltpu
from jax.sharding import PartitionSpec as P

GROUP = 32
DEPTH = 8 * GROUP
LINK = jnp.bfloat16
VMEM = pl.BlockSpec(memory_space=pltpu.VMEM)
HBM = pl.BlockSpec(memory_space=pltpu.HBM)


def in_hbm(*arrays):
    return [pltpu.with_memory_space_constraint(x, pltpu.HBM) for x in arrays]


def fetch(sources, targets, sems):
    copies = [pltpu.make_async_copy(s, t, sems.at[i]) for i, (s, t) in enumerate(zip(sources, targets))]
    for c in copies:
        c.start()
    return copies


def tile_of(n, most):
    while n % most:
        most //= 2
    return most


def column(row):
    n = row.shape[1]
    eye = lax.broadcasted_iota(jnp.int32, (n, n), 0) == lax.broadcasted_iota(jnp.int32, (n, n), 1)
    return jnp.sum(jnp.where(eye, row, jnp.zeros_like(row)), axis=1, keepdims=True)


def split3(x):
    first = x.astype(jnp.bfloat16).astype(jnp.float32)
    rest = x - first
    second = rest.astype(jnp.bfloat16).astype(jnp.float32)
    third = (rest - second).astype(jnp.bfloat16).astype(jnp.float32)
    return first, second, third


def pick_row(shape, rows):
    index = lax.broadcasted_iota(jnp.int32, shape, 0)
    out = jnp.zeros(shape, jnp.float32)
    for i, row in enumerate(rows):
        out = jnp.where(index == i, row, out)
    return out


def partial_kernel(n_col, swapped, n_more, *refs):
    sources, refs = refs[: 2 + n_more], refs[2 + n_more :]
    more, out_refs, (panel_ref, sems) = refs[: n_more + 1], refs[n_more + 1 : -2], refs[-2:]
    inv_ref = more[0]
    copies = fetch(sources, (panel_ref, *more), sems)
    rows = panel_ref.shape[0] // n_col
    me = lax.axis_index("col")
    for c in copies[:2]:
        c.wait()
    inv = inv_ref[...]
    panel = panel_ref[...]
    if swapped:
        panel = jnp.concatenate([panel_ref[pl.ds((me ^ d) * rows, rows), :] for d in range(n_col)], axis=0)
    slab = lax.dot_general(
        panel, inv, (((1,), (1,)), ((), ())), preferred_element_type=jnp.float32
    ).astype(jnp.bfloat16)
    part = jnp.dot(slab, inv, preferred_element_type=jnp.float32)
    if swapped:
        for d in range(n_col):
            out_refs[d][...] = part[d * rows : (d + 1) * rows].astype(out_refs[d].dtype)
    else:
        out_refs[0][...] = part.reshape(out_refs[0].shape).astype(out_refs[0].dtype)
    for c in copies[2:]:
        c.wait()


def partial(panel, inv, more, n_col, swapped):
    rows, width = panel.shape[0] // n_col, panel.shape[1]
    shapes = [jax.ShapeDtypeStruct(x.shape, x.dtype) for x in (inv, *more)]
    if swapped:
        shapes += [jax.ShapeDtypeStruct((rows, width), jnp.float32 if d == 0 else LINK) for d in range(n_col)]
    else:
        shapes += [jax.ShapeDtypeStruct((n_col, rows, width), LINK)]
    out = pl.pallas_call(
        functools.partial(partial_kernel, n_col, swapped, len(more)),
        out_shape=shapes,
        in_specs=[HBM] * (2 + len(more)),
        out_specs=[VMEM] * len(shapes),
        scratch_shapes=[pltpu.VMEM(panel.shape, panel.dtype), pltpu.SemaphoreType.DMA((2 + len(more),))],
        compiler_params=pltpu.CompilerParams(vmem_limit_bytes=16 * 2**20),
        name="partial",
    )(*in_hbm(panel, inv, *more))
    return out[: 1 + len(more)], out[1 + len(more) :]


def columns_kernel(
    tile, inv_ref, points_ref, scale_ref, target_ref, pick_ref, a_ref, b_ref,
    k_ref, sums_ref, p32, pwide, pt, s32, st,
):
    din, depth = points_ref.shape
    wide = a_ref.shape[1]
    block = wide // pick_ref.shape[0]
    p32[...] = jnp.zeros_like(p32)
    s32[...] = jnp.zeros_like(s32)
    st[...] = jnp.zeros_like(st)
    inverse = 1.0 / column(scale_ref[...])
    p32[:din, :] = (points_ref[...] - 0.5) * inverse
    p = p32[...]
    first, second, third = split3(p)
    for g, part in enumerate((first, first, second, second, first, third)):
        pwide[g * GROUP : (g + 1) * GROUP, :] = part
    norm = -0.5 * jnp.sum(p * p, axis=0, keepdims=True)
    minus = jnp.full_like(norm, -1.0)
    pwide[6 * GROUP : 7 * GROUP, :] = pick_row((GROUP, depth), (minus, minus, minus) + split3(norm))
    pwide[7 * GROUP :, :] = jnp.zeros((GROUP, depth), jnp.float32)
    pt[...] = jnp.transpose(pwide[...]).astype(jnp.bfloat16)
    weight = (
        jnp.sum(inv_ref[...].astype(jnp.float32) * target_ref[...].astype(jnp.float32).reshape(1, depth), axis=1, keepdims=True)
        .astype(jnp.bfloat16)
        .astype(jnp.float32)
    )

    def step(t, carry):
        cols = pl.ds(t * tile, tile)
        for i in range(tile // block):
            chosen = column(pick_ref[pl.ds(t * (tile // block) + i, 1), :])
            here = pl.ds(t * tile + i * block, block)
            s32[:din, i * block : (i + 1) * block] = (
                jnp.where(chosen == 1, b_ref[:, here], a_ref[:, here]) - 0.5
            ) * inverse
        s = s32[...]
        first, second, third = split3(s)
        for g, part in enumerate((first, second, first, second, third, first)):
            st[g * GROUP : (g + 1) * GROUP, :] = part.astype(jnp.bfloat16)
        norm = 0.5 * jnp.sum(s * s, axis=0, keepdims=True)
        one = jnp.ones_like(norm)
        st[6 * GROUP : 7 * GROUP, :] = pick_row((GROUP, tile), split3(norm) + (one, one, one)).astype(jnp.bfloat16)
        power = jnp.dot(pt[...], st[...], preferred_element_type=jnp.float32)
        k = jnp.exp(power).astype(jnp.bfloat16)
        k_ref[:, cols] = k
        solve = jnp.dot(inv_ref[...], k, preferred_element_type=jnp.float32)
        solve = solve.astype(jnp.bfloat16).astype(jnp.float32)
        sums_ref[0:1, cols] = jnp.sum(solve * weight, axis=0, keepdims=True)
        sums_ref[1:2, cols] = jnp.sum(solve * solve, axis=0, keepdims=True)
        return carry

    lax.fori_loop(0, wide // tile, step, 0, unroll=True)


def columns(ins):
    inv, points, _, _, picks, base, _ = ins
    depth, wide, blocks = points.shape[1], base.shape[1], picks.shape[0]
    tile = wide // blocks * (2 if blocks % 2 == 0 else 1)
    return pl.pallas_call(
        functools.partial(columns_kernel, tile),
        out_shape=[
            jax.ShapeDtypeStruct((depth, wide), jnp.bfloat16),
            jax.ShapeDtypeStruct((2, wide), jnp.float32),
        ],
        in_specs=[VMEM] * len(ins),
        out_specs=[VMEM] * 2,
        scratch_shapes=[
            pltpu.VMEM((GROUP, depth), jnp.float32),
            pltpu.VMEM((DEPTH, depth), jnp.float32),
            pltpu.VMEM((depth, DEPTH), jnp.bfloat16),
            pltpu.VMEM((GROUP, tile), jnp.float32),
            pltpu.VMEM((DEPTH, tile), jnp.bfloat16),
        ],
        compiler_params=pltpu.CompilerParams(vmem_limit_bytes=32 * 2**20),
        cost_estimate=pl.CostEstimate(
            flops=2 * depth * wide * (DEPTH + inv.shape[0]), bytes_accessed=2 * depth * wide, transcendentals=depth * wide
        ),
        name="columns",
    )(*ins)


def update_kernel(places, cuts, n_in, *refs):
    blocks, (k_ref, rhs_ref, panel_ref, trailing_ref) = refs[:n_in], refs[n_in : n_in + 4]
    cross_hbm, next_hbm, left, cross, following, sems = refs[n_in + 4 :]
    rows, wide = rhs_ref.shape
    me = lax.axis_index("row")
    for ref, place in zip(blocks, places):
        height = ref.shape[0] // len(place)
        for i, xor in enumerate(place):
            start = 0 if xor is None else (me ^ xor) * height
            left[pl.ds(start, height), :] = ref[i * height : (i + 1) * height, :]
    product = lax.dot_general(
        panel_ref[...], left[...], (((1,), (1,)), ((), ())), preferred_element_type=jnp.float32
    )
    following[...] = trailing_ref[...] - product
    copies = [pltpu.make_async_copy(following, next_hbm, sems.at[len(cuts)])]
    copies[0].start()
    for t, (start, stop) in enumerate(cuts):
        product = jnp.dot(left[...], k_ref[:, start:stop], preferred_element_type=jnp.float32)
        cross[:, start:stop] = (rhs_ref[:, start:stop].astype(jnp.float32) - product).astype(cross.dtype)
        copies.append(pltpu.make_async_copy(cross.at[:, start:stop], cross_hbm.at[:, start:stop], sems.at[t]))
        copies[-1].start()
    for c in copies:
        c.wait()


def update(blocks, places, k, rhs, panel, trailing):
    depth, wide = k.shape
    rows = rhs.shape[0]
    tile = tile_of(wide, 512)
    edges = list(range(0, wide, tile)) + [wide - tile // 2, wide]
    cuts = list(zip(edges, edges[1:]))
    return pl.pallas_call(
        functools.partial(update_kernel, places, cuts, len(blocks)),
        out_shape=[
            jax.ShapeDtypeStruct(rhs.shape, rhs.dtype),
            jax.ShapeDtypeStruct(trailing.shape, trailing.dtype),
        ],
        in_specs=[VMEM] * (len(blocks) + 4),
        out_specs=[HBM, HBM],
        scratch_shapes=[
            pltpu.VMEM((rows, depth), jnp.bfloat16),
            pltpu.VMEM(rhs.shape, rhs.dtype),
            pltpu.VMEM(trailing.shape, trailing.dtype),
            pltpu.SemaphoreType.DMA((len(cuts) + 1,)),
        ],
        compiler_params=pltpu.CompilerParams(vmem_limit_bytes=32 * 2**20),
        cost_estimate=pl.CostEstimate(
            flops=2 * rows * depth * wide, bytes_accessed=2 * depth * wide, transcendentals=0
        ),
        name="update",
    )(*blocks, k, rhs, panel, trailing)


def finish_kernel(*refs):
    parts, (mean_ref, var_ref, out_mean, out_var) = refs[:-4], refs[-4:]
    total = parts[0][...]
    for x in parts[1:]:
        total = total + x[...]
    out_mean[...] = mean_ref[...] + total[0:1]
    out_var[...] = var_ref[...] - total[1:2]


def finish(parts, mean, var):
    wide = mean.shape[0]
    flat = jax.ShapeDtypeStruct((1, wide), jnp.float32)
    out_mean, out_var = pl.pallas_call(
        finish_kernel,
        out_shape=[flat, flat],
        in_specs=[VMEM] * (len(parts) + 2),
        out_specs=[VMEM] * 2,
        compiler_params=pltpu.CompilerParams(vmem_limit_bytes=8 * 2**20),
        name="finish",
    )(*parts, mean.reshape(1, wide), var.reshape(1, wide))
    return out_mean.reshape(wide), out_var.reshape(wide)


def swap(x, axis, d):
    return lax.ppermute(x, axis, [(i, i ^ d) for i in range(lax.axis_size(axis))])


def local(
    trailing,
    panel_block,
    diag_inverse,
    panel_points,
    lengthscales,
    targets,
    base_a,
    base_b,
    pick_sets,
    cross_rhs,
    mean_in,
    var_in,
):
    n_row, n_col = lax.axis_size("row"), lax.axis_size("col")
    near = n_col in (2, 4)
    more = (panel_points, lengthscales.reshape(1, -1), targets, pick_sets, base_a, base_b)
    ins, parts = partial(panel_block, diag_inverse, more, n_col, near)
    if near:
        got = [swap(parts[d], "col", d) for d in (2, 3, 1) if d < n_col]
    k, sums = columns(ins)
    if near:
        got, k, sums = lax.optimization_barrier((got, k, sums))
        reduced = parts[0]
        for x in got:
            reduced = reduced + x.astype(jnp.float32)
        totals = [sums] + [swap(sums, "col", d) for d in range(1, n_col)]
    else:
        reduced = lax.all_to_all(parts[0], "col", 0, 0).astype(jnp.float32).sum(0)
        totals = [lax.psum(sums, "col")]
    reduced = reduced.astype(LINK)
    if n_row == 8:
        pair = jnp.concatenate([reduced, swap(reduced, "row", 1)], axis=0)
        blocks = [pair] + [swap(pair, "row", d) for d in (2, 4, 6)]
        places = [(d, d + 1) for d in (0, 2, 4, 6)]
    else:
        blocks, places = [lax.all_gather(reduced, "row", axis=0, tiled=True)], [(None,)]
    cross_next, trailing_next = update(blocks, places, k, cross_rhs, panel_block, trailing)
    cross_next, totals = lax.optimization_barrier((cross_next, totals))
    return trailing_next, cross_next, *finish(totals, mean_in, var_in)


def solution(mesh):
    placed = (
        P("row", "col"),
        P("row", None),
        P("col", None),
        P(),
        P(),
        P(),
        P(None, "row"),
        P(None, "row"),
        P("row", None),
        P("col", "row"),
        P("row"),
        P("row"),
    )
    return jax.shard_map(
        local,
        mesh=mesh,
        in_specs=placed,
        out_specs=(P("row", "col"), P("col", "row"), P("row"), P("row")),
        check_vma=False,
    )
```

```python
import functools

import jax
import jax.numpy as jnp
from jax import lax
from jax.experimental import pallas as pl
from jax.experimental.pallas import tpu as pltpu
from jax.sharding import PartitionSpec as P

GROUP = 32
DEPTH = 8 * GROUP
LINK = jnp.bfloat16
VMEM = pl.BlockSpec(memory_space=pltpu.VMEM)
HBM = pl.BlockSpec(memory_space=pltpu.HBM)


def in_hbm(*arrays):
    return [pltpu.with_memory_space_constraint(x, pltpu.HBM) for x in arrays]


def fetch(sources, targets, sems):
    copies = [pltpu.make_async_copy(s, t, sems.at[i]) for i, (s, t) in enumerate(zip(sources, targets))]
    for c in copies:
        c.start()
    return copies


def tile_of(n, most):
    while n % most:
        most //= 2
    return most


def column(row):
    n = row.shape[1]
    eye = lax.broadcasted_iota(jnp.int32, (n, n), 0) == lax.broadcasted_iota(jnp.int32, (n, n), 1)
    return jnp.sum(jnp.where(eye, row, jnp.zeros_like(row)), axis=1, keepdims=True)


def split3(x):
    first = x.astype(jnp.bfloat16).astype(jnp.float32)
    rest = x - first
    second = rest.astype(jnp.bfloat16).astype(jnp.float32)
    third = (rest - second).astype(jnp.bfloat16).astype(jnp.float32)
    return first, second, third


def pick_row(shape, rows):
    index = lax.broadcasted_iota(jnp.int32, shape, 0)
    out = jnp.zeros(shape, jnp.float32)
    for i, row in enumerate(rows):
        out = jnp.where(index == i, row, out)
    return out


def partial_kernel(n_col, swapped, n_more, *refs):
    sources, refs = refs[: 2 + n_more], refs[2 + n_more :]
    more, pt, out_refs = refs[:n_more], refs[n_more], refs[n_more + 1 : -5]
    panel_ref, points_ref, p32, pwide, sems = refs[-5:]
    inv_ref, scale_ref = more[:2]
    din, depth = points_ref.shape
    order = (2, 3, 0, 1, 4, 5, 6, 7)
    targets = (panel_ref, inv_ref, points_ref, *more[1:])
    copies = fetch([sources[i] for i in order], [targets[i] for i in order], sems)
    rows = panel_ref.shape[0] // n_col
    me = lax.axis_index("col")
    p32[...] = jnp.zeros_like(p32)
    for c in copies[:2]:
        c.wait()
    inverse = 1.0 / column(scale_ref[...])
    p32[:din, :] = (points_ref[...] - 0.5) * inverse
    p = p32[...]
    first, second, third = split3(p)
    for g, part in enumerate((first, first, second, second, first, third)):
        pwide[g * GROUP : (g + 1) * GROUP, :] = part
    norm = -0.5 * jnp.sum(p * p, axis=0, keepdims=True)
    minus = jnp.full_like(norm, -1.0)
    pwide[6 * GROUP : 7 * GROUP, :] = pick_row((GROUP, depth), (minus, minus, minus) + split3(norm))
    pwide[7 * GROUP :, :] = jnp.zeros((GROUP, depth), jnp.float32)
    pt[...] = jnp.transpose(pwide[...]).astype(jnp.bfloat16)
    for c in copies[2:4]:
        c.wait()
    inv = inv_ref[...]
    panel = panel_ref[...]
    if swapped:
        panel = jnp.concatenate([panel_ref[pl.ds((me ^ d) * rows, rows), :] for d in range(n_col)], axis=0)
    slab = lax.dot_general(
        panel, inv, (((1,), (1,)), ((), ())), preferred_element_type=jnp.float32
    ).astype(jnp.bfloat16)
    part = jnp.dot(slab, inv, preferred_element_type=jnp.float32)
    if swapped:
        for d in range(n_col):
            out_refs[d][...] = part[d * rows : (d + 1) * rows].astype(out_refs[d].dtype)
    else:
        out_refs[0][...] = part.reshape(out_refs[0].shape).astype(out_refs[0].dtype)
    for c in copies[4:]:
        c.wait()


def partial(panel, inv, more, n_col, swapped):
    rows, width = panel.shape[0] // n_col, panel.shape[1]
    points = more[0]
    shapes = [jax.ShapeDtypeStruct(x.shape, x.dtype) for x in (inv, *more[1:])]
    shapes += [jax.ShapeDtypeStruct((points.shape[1], DEPTH), jnp.bfloat16)]
    if swapped:
        shapes += [jax.ShapeDtypeStruct((rows, width), jnp.float32 if d == 0 else LINK) for d in range(n_col)]
    else:
        shapes += [jax.ShapeDtypeStruct((n_col, rows, width), LINK)]
    out = pl.pallas_call(
        functools.partial(partial_kernel, n_col, swapped, len(more)),
        out_shape=shapes,
        in_specs=[HBM] * (2 + len(more)),
        out_specs=[VMEM] * len(shapes),
        scratch_shapes=[
            pltpu.VMEM(panel.shape, panel.dtype),
            pltpu.VMEM(points.shape, points.dtype),
            pltpu.VMEM((GROUP, points.shape[1]), jnp.float32),
            pltpu.VMEM((DEPTH, points.shape[1]), jnp.float32),
            pltpu.SemaphoreType.DMA((2 + len(more),)),
        ],
        compiler_params=pltpu.CompilerParams(vmem_limit_bytes=16 * 2**20),
        name="partial",
    )(*in_hbm(panel, inv, *more))
    return out[: 1 + len(more)], out[1 + len(more) :]


def columns_kernel(
    tile, inv_ref, scale_ref, target_ref, pick_ref, a_ref, b_ref, pt,
    k_ref, sums_ref, s32, st,
):
    din, depth = a_ref.shape[0], pt.shape[0]
    wide = a_ref.shape[1]
    block = wide // pick_ref.shape[0]
    s32[...] = jnp.zeros_like(s32)
    st[...] = jnp.zeros_like(st)
    inverse = 1.0 / column(scale_ref[...])
    weight = (
        jnp.sum(inv_ref[...].astype(jnp.float32) * target_ref[...].astype(jnp.float32).reshape(1, depth), axis=1, keepdims=True)
        .astype(jnp.bfloat16)
        .astype(jnp.float32)
    )

    def step(t, carry):
        cols = pl.ds(t * tile, tile)
        for i in range(tile // block):
            chosen = column(pick_ref[pl.ds(t * (tile // block) + i, 1), :])
            here = pl.ds(t * tile + i * block, block)
            s32[:din, i * block : (i + 1) * block] = (
                jnp.where(chosen == 1, b_ref[:, here], a_ref[:, here]) - 0.5
            ) * inverse
        s = s32[...]
        first, second, third = split3(s)
        for g, part in enumerate((first, second, first, second, third, first)):
            st[g * GROUP : (g + 1) * GROUP, :] = part.astype(jnp.bfloat16)
        norm = 0.5 * jnp.sum(s * s, axis=0, keepdims=True)
        one = jnp.ones_like(norm)
        st[6 * GROUP : 7 * GROUP, :] = pick_row((GROUP, tile), split3(norm) + (one, one, one)).astype(jnp.bfloat16)
        power = jnp.dot(pt[...], st[...], preferred_element_type=jnp.float32)
        k = jnp.exp(power).astype(jnp.bfloat16)
        k_ref[:, cols] = k
        solve = jnp.dot(inv_ref[...], k, preferred_element_type=jnp.float32)
        solve = solve.astype(jnp.bfloat16).astype(jnp.float32)
        sums_ref[0:1, cols] = jnp.sum(solve * weight, axis=0, keepdims=True)
        sums_ref[1:2, cols] = jnp.sum(solve * solve, axis=0, keepdims=True)
        return carry

    lax.fori_loop(0, wide // tile, step, 0, unroll=True)


def columns(ins):
    inv, _, _, picks, base, _, pt = ins
    din, depth, wide, blocks = base.shape[0], pt.shape[0], base.shape[1], picks.shape[0]
    tile = wide // blocks * (4 if blocks % 4 == 0 else 1)
    return pl.pallas_call(
        functools.partial(columns_kernel, tile),
        out_shape=[
            jax.ShapeDtypeStruct((depth, wide), jnp.bfloat16),
            jax.ShapeDtypeStruct((2, wide), jnp.float32),
        ],
        in_specs=[VMEM] * len(ins),
        out_specs=[VMEM] * 2,
        scratch_shapes=[
            pltpu.VMEM((GROUP, tile), jnp.float32),
            pltpu.VMEM((DEPTH, tile), jnp.bfloat16),
        ],
        compiler_params=pltpu.CompilerParams(vmem_limit_bytes=32 * 2**20),
        cost_estimate=pl.CostEstimate(
            flops=2 * depth * wide * (DEPTH + inv.shape[0]), bytes_accessed=2 * depth * wide, transcendentals=depth * wide
        ),
        name="columns",
    )(*ins)


def update_kernel(places, cuts, n_in, *refs):
    blocks, (k_ref, rhs_ref, panel_ref, trailing_ref) = refs[:n_in], refs[n_in : n_in + 4]
    cross_hbm, next_hbm, left, cross, following, sems = refs[n_in + 4 :]
    rows, wide = rhs_ref.shape
    me = lax.axis_index("row")
    for ref, place in zip(blocks, places):
        height = ref.shape[0] // len(place)
        for i, xor in enumerate(place):
            start = 0 if xor is None else (me ^ xor) * height
            left[pl.ds(start, height), :] = ref[i * height : (i + 1) * height, :]
    product = lax.dot_general(
        panel_ref[...], left[...], (((1,), (1,)), ((), ())), preferred_element_type=jnp.float32
    )
    following[...] = trailing_ref[...] - product
    copies = [pltpu.make_async_copy(following, next_hbm, sems.at[len(cuts)])]
    copies[0].start()
    for t, (start, stop) in enumerate(cuts):
        product = jnp.dot(left[...], k_ref[:, start:stop], preferred_element_type=jnp.float32)
        cross[:, start:stop] = (rhs_ref[:, start:stop].astype(jnp.float32) - product).astype(cross.dtype)
        copies.append(pltpu.make_async_copy(cross.at[:, start:stop], cross_hbm.at[:, start:stop], sems.at[t]))
        copies[-1].start()
    for c in copies:
        c.wait()


def update(blocks, places, k, rhs, panel, trailing):
    depth, wide = k.shape
    rows = rhs.shape[0]
    tile = tile_of(wide, 512)
    edges = list(range(0, wide, tile)) + [wide - tile // 2, wide]
    cuts = list(zip(edges, edges[1:]))
    return pl.pallas_call(
        functools.partial(update_kernel, places, cuts, len(blocks)),
        out_shape=[
            jax.ShapeDtypeStruct(rhs.shape, rhs.dtype),
            jax.ShapeDtypeStruct(trailing.shape, trailing.dtype),
        ],
        in_specs=[VMEM] * (len(blocks) + 4),
        out_specs=[HBM, HBM],
        scratch_shapes=[
            pltpu.VMEM((rows, depth), jnp.bfloat16),
            pltpu.VMEM(rhs.shape, rhs.dtype),
            pltpu.VMEM(trailing.shape, trailing.dtype),
            pltpu.SemaphoreType.DMA((len(cuts) + 1,)),
        ],
        compiler_params=pltpu.CompilerParams(vmem_limit_bytes=32 * 2**20),
        cost_estimate=pl.CostEstimate(
            flops=2 * rows * depth * wide, bytes_accessed=2 * depth * wide, transcendentals=0
        ),
        name="update",
    )(*blocks, k, rhs, panel, trailing)


def finish_kernel(*refs):
    parts, (mean_ref, var_ref, out_mean, out_var) = refs[:-4], refs[-4:]
    total = parts[0][...]
    for x in parts[1:]:
        total = total + x[...]
    out_mean[...] = mean_ref[...] + total[0:1]
    out_var[...] = var_ref[...] - total[1:2]


def finish(parts, mean, var):
    wide = mean.shape[0]
    flat = jax.ShapeDtypeStruct((1, wide), jnp.float32)
    out_mean, out_var = pl.pallas_call(
        finish_kernel,
        out_shape=[flat, flat],
        in_specs=[VMEM] * (len(parts) + 2),
        out_specs=[VMEM] * 2,
        compiler_params=pltpu.CompilerParams(vmem_limit_bytes=8 * 2**20),
        name="finish",
    )(*parts, mean.reshape(1, wide), var.reshape(1, wide))
    return out_mean.reshape(wide), out_var.reshape(wide)


def swap(x, axis, d):
    return lax.ppermute(x, axis, [(i, i ^ d) for i in range(lax.axis_size(axis))])


def local(
    trailing,
    panel_block,
    diag_inverse,
    panel_points,
    lengthscales,
    targets,
    base_a,
    base_b,
    pick_sets,
    cross_rhs,
    mean_in,
    var_in,
):
    n_row, n_col = lax.axis_size("row"), lax.axis_size("col")
    near = n_col in (2, 4)
    more = (panel_points, lengthscales.reshape(1, -1), targets, pick_sets, base_a, base_b)
    ins, parts = partial(panel_block, diag_inverse, more, n_col, near)
    if near:
        got = [swap(parts[d], "col", d) for d in (2, 3, 1) if d < n_col]
    k, sums = columns(ins)
    if near:
        got, k, sums = lax.optimization_barrier((got, k, sums))
        reduced = parts[0]
        for x in got:
            reduced = reduced + x.astype(jnp.float32)
        totals = [sums] + [swap(sums, "col", d) for d in range(1, n_col)]
    else:
        reduced = lax.all_to_all(parts[0], "col", 0, 0).astype(jnp.float32).sum(0)
        totals = [lax.psum(sums, "col")]
    reduced = reduced.astype(LINK)
    if n_row == 8:
        pair = jnp.concatenate([reduced, swap(reduced, "row", 1)], axis=0)
        blocks = [pair] + [swap(pair, "row", d) for d in (2, 4, 6)]
        places = [(d, d + 1) for d in (0, 2, 4, 6)]
    else:
        blocks, places = [lax.all_gather(reduced, "row", axis=0, tiled=True)], [(None,)]
    cross_next, trailing_next = update(blocks, places, k, cross_rhs, panel_block, trailing)
    cross_next, totals = lax.optimization_barrier((cross_next, totals))
    return trailing_next, cross_next, *finish(totals, mean_in, var_in)


def solution(mesh):
    placed = (
        P("row", "col"),
        P("row", None),
        P("col", None),
        P(),
        P(),
        P(),
        P(None, "row"),
        P(None, "row"),
        P("row", None),
        P("col", "row"),
        P("row"),
        P("row"),
    )
    return jax.shard_map(
        local,
        mesh=mesh,
        in_specs=placed,
        out_specs=(P("row", "col"), P("col", "row"), P("row"), P("row")),
        check_vma=False,
    )
```

```python
import functools

import jax
import jax.numpy as jnp
from jax import lax
from jax.experimental import pallas as pl
from jax.experimental.pallas import tpu as pltpu
from jax.sharding import PartitionSpec as P

GROUP = 32
DEPTH = 8 * GROUP
LINK = jnp.bfloat16
VMEM = pl.BlockSpec(memory_space=pltpu.VMEM)
HBM = pl.BlockSpec(memory_space=pltpu.HBM)


def in_hbm(*arrays):
    return [pltpu.with_memory_space_constraint(x, pltpu.HBM) for x in arrays]


def fetch(sources, targets, sems):
    copies = [pltpu.make_async_copy(s, t, sems.at[i]) for i, (s, t) in enumerate(zip(sources, targets))]
    for c in copies:
        c.start()
    return copies


def turns(n_col):
    return [tuple(d for d in order if d < n_col) for order in ((2, 3, 1), (3, 1, 2))]


def tile_of(n, most):
    while n % most:
        most //= 2
    return most


def column(row):
    n = row.shape[1]
    eye = lax.broadcasted_iota(jnp.int32, (n, n), 0) == lax.broadcasted_iota(jnp.int32, (n, n), 1)
    return jnp.sum(jnp.where(eye, row, jnp.zeros_like(row)), axis=1, keepdims=True)


def split3(x):
    first = x.astype(jnp.bfloat16).astype(jnp.float32)
    rest = x - first
    second = rest.astype(jnp.bfloat16).astype(jnp.float32)
    third = (rest - second).astype(jnp.bfloat16).astype(jnp.float32)
    return first, second, third


def pick_row(shape, rows):
    index = lax.broadcasted_iota(jnp.int32, shape, 0)
    out = jnp.zeros(shape, jnp.float32)
    for i, row in enumerate(rows):
        out = jnp.where(index == i, row, out)
    return out


def partial_kernel(n_col, swapped, n_more, *refs):
    sources, refs = refs[: 2 + n_more], refs[2 + n_more :]
    more, pt, out_refs = refs[:n_more], refs[n_more], refs[n_more + 1 : -5]
    panel_ref, points_ref, p32, pwide, sems = refs[-5:]
    inv_ref, scale_ref = more[:2]
    din, depth = points_ref.shape
    order = (2, 3, 0, 1, 4, 5, 6, 7)
    targets = (panel_ref, inv_ref, points_ref, *more[1:])
    copies = fetch([sources[i] for i in order], [targets[i] for i in order], sems)
    rows = panel_ref.shape[0] // n_col
    me = lax.axis_index("col")
    p32[...] = jnp.zeros_like(p32)
    for c in copies[:2]:
        c.wait()
    inverse = 1.0 / column(scale_ref[...])
    p32[:din, :] = (points_ref[...] - 0.5) * inverse
    p = p32[...]
    first, second, third = split3(p)
    for g, part in enumerate((first, first, second, second, first, third)):
        pwide[g * GROUP : (g + 1) * GROUP, :] = part
    norm = -0.5 * jnp.sum(p * p, axis=0, keepdims=True)
    minus = jnp.full_like(norm, -1.0)
    pwide[6 * GROUP : 7 * GROUP, :] = pick_row((GROUP, depth), (minus, minus, minus) + split3(norm))
    pwide[7 * GROUP :, :] = jnp.zeros((GROUP, depth), jnp.float32)
    pt[...] = jnp.transpose(pwide[...]).astype(jnp.bfloat16)
    for c in copies[2:4]:
        c.wait()
    inv = inv_ref[...]
    panel = panel_ref[...]
    if swapped:
        odd = lax.axis_index("row") % 2
        steps = [0] + [jnp.where(odd == 1, b, a) for a, b in zip(*turns(n_col))]
        panel = jnp.concatenate([panel_ref[pl.ds((me ^ d) * rows, rows), :] for d in steps], axis=0)
    slab = lax.dot_general(
        panel, inv, (((1,), (1,)), ((), ())), preferred_element_type=jnp.float32
    ).astype(jnp.bfloat16)
    part = jnp.dot(slab, inv, preferred_element_type=jnp.float32)
    if swapped:
        for d in range(n_col):
            out_refs[d][...] = part[d * rows : (d + 1) * rows].astype(out_refs[d].dtype)
    else:
        out_refs[0][...] = part.reshape(out_refs[0].shape).astype(out_refs[0].dtype)
    for c in copies[4:]:
        c.wait()


def partial(panel, inv, more, n_col, swapped):
    rows, width = panel.shape[0] // n_col, panel.shape[1]
    points = more[0]
    shapes = [jax.ShapeDtypeStruct(x.shape, x.dtype) for x in (inv, *more[1:])]
    shapes += [jax.ShapeDtypeStruct((points.shape[1], DEPTH), jnp.bfloat16)]
    if swapped:
        shapes += [jax.ShapeDtypeStruct((rows, width), jnp.float32 if d == 0 else LINK) for d in range(n_col)]
    else:
        shapes += [jax.ShapeDtypeStruct((n_col, rows, width), LINK)]
    out = pl.pallas_call(
        functools.partial(partial_kernel, n_col, swapped, len(more)),
        out_shape=shapes,
        in_specs=[HBM] * (2 + len(more)),
        out_specs=[VMEM] * len(shapes),
        scratch_shapes=[
            pltpu.VMEM(panel.shape, panel.dtype),
            pltpu.VMEM(points.shape, points.dtype),
            pltpu.VMEM((GROUP, points.shape[1]), jnp.float32),
            pltpu.VMEM((DEPTH, points.shape[1]), jnp.float32),
            pltpu.SemaphoreType.DMA((2 + len(more),)),
        ],
        compiler_params=pltpu.CompilerParams(vmem_limit_bytes=16 * 2**20),
        name="partial",
    )(*in_hbm(panel, inv, *more))
    return out[: 1 + len(more)], out[1 + len(more) :]


def columns_kernel(
    tile, inv_ref, scale_ref, target_ref, pick_ref, a_ref, b_ref, pt,
    k_ref, sums_ref, s32, st,
):
    din, depth = a_ref.shape[0], pt.shape[0]
    wide = a_ref.shape[1]
    block = wide // pick_ref.shape[0]
    s32[...] = jnp.zeros_like(s32)
    st[...] = jnp.zeros_like(st)
    inverse = 1.0 / column(scale_ref[...])
    weight = (
        jnp.sum(inv_ref[...].astype(jnp.float32) * target_ref[...].astype(jnp.float32).reshape(1, depth), axis=1, keepdims=True)
        .astype(jnp.bfloat16)
        .astype(jnp.float32)
    )

    def step(t, carry):
        cols = pl.ds(t * tile, tile)
        for i in range(tile // block):
            chosen = column(pick_ref[pl.ds(t * (tile // block) + i, 1), :])
            here = pl.ds(t * tile + i * block, block)
            s32[:din, i * block : (i + 1) * block] = (
                jnp.where(chosen == 1, b_ref[:, here], a_ref[:, here]) - 0.5
            ) * inverse
        s = s32[...]
        first, second, third = split3(s)
        for g, part in enumerate((first, second, first, second, third, first)):
            st[g * GROUP : (g + 1) * GROUP, :] = part.astype(jnp.bfloat16)
        norm = 0.5 * jnp.sum(s * s, axis=0, keepdims=True)
        one = jnp.ones_like(norm)
        st[6 * GROUP : 7 * GROUP, :] = pick_row((GROUP, tile), split3(norm) + (one, one, one)).astype(jnp.bfloat16)
        power = jnp.dot(pt[...], st[...], preferred_element_type=jnp.float32)
        k = jnp.exp(power).astype(jnp.bfloat16)
        k_ref[:, cols] = k
        solve = jnp.dot(inv_ref[...], k, preferred_element_type=jnp.float32)
        solve = solve.astype(jnp.bfloat16).astype(jnp.float32)
        sums_ref[0:1, cols] = jnp.sum(solve * weight, axis=0, keepdims=True)
        sums_ref[1:2, cols] = jnp.sum(solve * solve, axis=0, keepdims=True)
        return carry

    lax.fori_loop(0, wide // tile, step, 0, unroll=True)


def columns(ins):
    inv, _, _, picks, base, _, pt = ins
    din, depth, wide, blocks = base.shape[0], pt.shape[0], base.shape[1], picks.shape[0]
    tile = wide // blocks * (4 if blocks % 4 == 0 else 1)
    return pl.pallas_call(
        functools.partial(columns_kernel, tile),
        out_shape=[
            jax.ShapeDtypeStruct((depth, wide), jnp.bfloat16),
            jax.ShapeDtypeStruct((2, wide), jnp.float32),
        ],
        in_specs=[VMEM] * len(ins),
        out_specs=[VMEM] * 2,
        scratch_shapes=[
            pltpu.VMEM((GROUP, tile), jnp.float32),
            pltpu.VMEM((DEPTH, tile), jnp.bfloat16),
        ],
        compiler_params=pltpu.CompilerParams(vmem_limit_bytes=32 * 2**20),
        cost_estimate=pl.CostEstimate(
            flops=2 * depth * wide * (DEPTH + inv.shape[0]), bytes_accessed=2 * depth * wide, transcendentals=depth * wide
        ),
        name="columns",
    )(*ins)


def update_kernel(places, cuts, n_in, *refs):
    blocks, (k_ref, rhs_ref, panel_ref, trailing_ref) = refs[:n_in], refs[n_in : n_in + 4]
    cross_hbm, next_hbm, left, cross, following, sems = refs[n_in + 4 :]
    rows, wide = rhs_ref.shape
    me = lax.axis_index("row")
    for ref, place in zip(blocks, places):
        height = ref.shape[0] // len(place)
        for i, xor in enumerate(place):
            start = 0 if xor is None else (me ^ xor) * height
            left[pl.ds(start, height), :] = ref[i * height : (i + 1) * height, :]
    product = lax.dot_general(
        panel_ref[...], left[...], (((1,), (1,)), ((), ())), preferred_element_type=jnp.float32
    )
    following[...] = trailing_ref[...] - product
    copies = [pltpu.make_async_copy(following, next_hbm, sems.at[len(cuts)])]
    copies[0].start()
    for t, (start, stop) in enumerate(cuts):
        product = jnp.dot(left[...], k_ref[:, start:stop], preferred_element_type=jnp.float32)
        cross[:, start:stop] = (rhs_ref[:, start:stop].astype(jnp.float32) - product).astype(cross.dtype)
        copies.append(pltpu.make_async_copy(cross.at[:, start:stop], cross_hbm.at[:, start:stop], sems.at[t]))
        copies[-1].start()
    for c in copies:
        c.wait()


def update(blocks, places, k, rhs, panel, trailing):
    depth, wide = k.shape
    rows = rhs.shape[0]
    tile = tile_of(wide, 1024)
    edges = list(range(0, wide, tile)) + [wide - tile // 2, wide]
    cuts = list(zip(edges, edges[1:]))
    return pl.pallas_call(
        functools.partial(update_kernel, places, cuts, len(blocks)),
        out_shape=[
            jax.ShapeDtypeStruct(rhs.shape, rhs.dtype),
            jax.ShapeDtypeStruct(trailing.shape, trailing.dtype),
        ],
        in_specs=[VMEM] * (len(blocks) + 4),
        out_specs=[HBM, HBM],
        scratch_shapes=[
            pltpu.VMEM((rows, depth), jnp.bfloat16),
            pltpu.VMEM(rhs.shape, rhs.dtype),
            pltpu.VMEM(trailing.shape, trailing.dtype),
            pltpu.SemaphoreType.DMA((len(cuts) + 1,)),
        ],
        compiler_params=pltpu.CompilerParams(vmem_limit_bytes=32 * 2**20),
        cost_estimate=pl.CostEstimate(
            flops=2 * rows * depth * wide, bytes_accessed=2 * depth * wide, transcendentals=0
        ),
        name="update",
    )(*blocks, k, rhs, panel, trailing)


def finish_kernel(*refs):
    parts, (mean_ref, var_ref, out_mean, out_var) = refs[:-4], refs[-4:]
    total = parts[0][...]
    for x in parts[1:]:
        total = total + x[...]
    out_mean[...] = mean_ref[...] + total[0:1]
    out_var[...] = var_ref[...] - total[1:2]


def finish(parts, mean, var):
    wide = mean.shape[0]
    flat = jax.ShapeDtypeStruct((1, wide), jnp.float32)
    out_mean, out_var = pl.pallas_call(
        finish_kernel,
        out_shape=[flat, flat],
        in_specs=[VMEM] * (len(parts) + 2),
        out_specs=[VMEM] * 2,
        compiler_params=pltpu.CompilerParams(vmem_limit_bytes=8 * 2**20),
        name="finish",
    )(*parts, mean.reshape(1, wide), var.reshape(1, wide))
    return out_mean.reshape(wide), out_var.reshape(wide)


def meet(x, a, b):
    n_row, n_col = lax.axis_size("row"), lax.axis_size("col")
    pairs = [(r * n_col + c, r * n_col + (c ^ (b if r % 2 else a))) for r in range(n_row) for c in range(n_col)]
    return lax.ppermute(x, ("row", "col"), pairs)


def swap(x, axis, d):
    return lax.ppermute(x, axis, [(i, i ^ d) for i in range(lax.axis_size(axis))])


def local(
    trailing,
    panel_block,
    diag_inverse,
    panel_points,
    lengthscales,
    targets,
    base_a,
    base_b,
    pick_sets,
    cross_rhs,
    mean_in,
    var_in,
):
    n_row, n_col = lax.axis_size("row"), lax.axis_size("col")
    near = n_col in (2, 4)
    more = (panel_points, lengthscales.reshape(1, -1), targets, pick_sets, base_a, base_b)
    ins, parts = partial(panel_block, diag_inverse, more, n_col, near)
    if near:
        got = [meet(x, a, b) for x, a, b in zip(parts[1:], *turns(n_col))]
    k, sums = columns(ins)
    if near:
        got, k, sums = lax.optimization_barrier((got, k, sums))
        reduced = parts[0]
        for x in got:
            reduced = reduced + x.astype(jnp.float32)
        totals = [sums] + [swap(sums, "col", d) for d in range(1, n_col)]
    else:
        reduced = lax.all_to_all(parts[0], "col", 0, 0).astype(jnp.float32).sum(0)
        totals = [lax.psum(sums, "col")]
    reduced = reduced.astype(LINK)
    if n_row == 8:
        pair = jnp.concatenate([reduced, swap(reduced, "row", 1)], axis=0)
        blocks = [pair] + [swap(pair, "row", d) for d in (2, 4, 6)]
        places = [(d, d + 1) for d in (0, 2, 4, 6)]
    else:
        blocks, places = [lax.all_gather(reduced, "row", axis=0, tiled=True)], [(None,)]
    cross_next, trailing_next = update(blocks, places, k, cross_rhs, panel_block, trailing)
    cross_next, totals = lax.optimization_barrier((cross_next, totals))
    return trailing_next, cross_next, *finish(totals, mean_in, var_in)


def solution(mesh):
    placed = (
        P("row", "col"),
        P("row", None),
        P("col", None),
        P(),
        P(),
        P(),
        P(None, "row"),
        P(None, "row"),
        P("row", None),
        P("col", "row"),
        P("row"),
        P("row"),
    )
    return jax.shard_map(
        local,
        mesh=mesh,
        in_specs=placed,
        out_specs=(P("row", "col"), P("col", "row"), P("row"), P("row")),
        check_vma=False,
    )
```
